1024 devices in a mesh: board: 256 (over y, z, core), seq: 4 (over x).
Axes of the slice: x: 4, y: 8, z: 16, core: 2. Of those that a mesh axis runs over, the one named last changes fastest.
Arguments:
- board_cards: int32 [256, 6, 5], P('board'), may hold values from 0 to 51, as said below
- hand_ranks: int32 [256, 6, 1326], P('board'), may hold values from 0 to 7461
- river_count: int32 [256], P('board'), may hold values from 1 to 6, as said below
- reach_in: bfloat16 [256, 24, 1326], P('board', 'seq'), may hold values from 0 to 1
- strategy: bfloat16 [256, 6, 192, 1326], P('board', None, 'seq'), may hold values from 0.049804688 to 1
- parent_node: int32 [192], P('seq'), may hold values from 0 to 23, as said below
- pot_size: float32 [192], P('seq'), may hold values from 0.5 to 4
- flop_weight: float32 [256], P('board'), may hold values from 0.1 to 10
Outputs:
- turn_value: float32 [256, 24, 1326], P('board', 'seq')
- root_value: float32 [24, 1326], P('seq')
The draws below stay inside these ranges and needn't reach their ends.
Inputs may be any that keep to these rules, and one draw needn't show every extreme that they name: `board_cards`: the five cards of a river board are distinct; the first three are the flop group's and the same on all of its river boards. `river_count`: some flop group has 6 live river boards; slots at or past the count hold unused data. `parent_node`: each river root is the parent of exactly 8 leaves.
All inputs are finite; a program needn't handle non-finite values.
Results may differ from the reference program's by a relative error of at most 0.0003.
Values may be sent and summed in bfloat16 or wider, within the bound.
A program may use at most 32 MiB of HBM per device.

```python
import math
import jax
import jax.numpy as jnp
import numpy as np
from jax import lax

DECK = 52
HANDS = 1326
RIVERS = 6
NODES = 24
LEAVES = 192
BOARDS = 256


def draw_board_cards(key, part):

    def flop_group(group_key):
        key_flop, key_river = jax.random.split(group_key)
        shuffled = jax.random.permutation(key_flop, DECK)
        flop_cards = shuffled[:3]
        remaining = shuffled[3:]

        def one_river(river_key):
            chosen = jax.random.permutation(river_key, DECK - 3)[:2]
            return jnp.concatenate([flop_cards, remaining[chosen]])
        return jax.vmap(one_river)(jax.random.split(key_river, RIVERS))
    return jax.vmap(flop_group)(jax.random.split(key, BOARDS)).astype(jnp.int32)


def draw_river_count(key, part):
    key_one, key_two, key_top = jax.random.split(jax.random.fold_in(key, 17), 3)
    factor_one = jax.random.randint(key_one, (BOARDS,), 0, RIVERS)
    factor_two = jax.random.randint(key_two, (BOARDS,), 0, RIVERS)
    counted = 1 + factor_one * factor_two // (RIVERS - 1)
    busiest = jax.random.randint(key_top, (), 0, BOARDS)
    counted = jnp.where(jnp.arange(BOARDS) == busiest, RIVERS, counted)
    return counted.astype(jnp.int32)


def draw_parent_node(key, part):
    shuffled = jax.random.permutation(jax.random.fold_in(key, 29), LEAVES)
    return (shuffled % NODES).astype(jnp.int32)


def touch_ends(drawn, key, low, largest):
    longest = drawn.shape.index(max(drawn.shape))
    spots = []
    for shift in (0, 1):
        where = [jax.random.randint(jax.random.fold_in(key, axis), (), 0, length) for axis, length in enumerate(drawn.shape)]
        where[longest] = (where[longest] + shift) % drawn.shape[longest]
        spots.append(tuple(where))
    return drawn.at[spots[0]].set(low).at[spots[1]].set(largest)


def levels(stream_key, dims, shards, low, top_value):
    def one(axis_at, parts):
        heights = jax.random.uniform(jax.random.fold_in(jax.random.fold_in(stream_key, 6), axis_at), (parts,), jnp.float32, low / len(shards), top_value / len(shards))
        return jnp.repeat(jnp.exp(heights), dims[axis_at] // parts).reshape((-1,) + (1,) * (len(dims) - axis_at - 1))

    loudness = one(*shards[0])
    for cut in shards[1:]:
        loudness = loudness * one(*cut)
    return loudness


def setup_inputs(seed: int = 0) -> dict:
    streams_of = jax.random.split(jax.random.key(seed), 9)
    return {
        "board_cards": draw_board_cards(jax.random.fold_in(streams_of[8], 71), 0),
        "hand_ranks": touch_ends(jax.random.randint(streams_of[1], (BOARDS, RIVERS, HANDS), 0, 7462), jax.random.fold_in(streams_of[1], 1), 0, 7461).astype(jnp.int32),
        "river_count": draw_river_count(jax.random.fold_in(streams_of[8], 71), 0),
        "reach_in": jnp.clip(1.0 * jax.random.uniform(streams_of[3], (BOARDS, NODES, HANDS), jnp.float32) ** levels(streams_of[3], (BOARDS, NODES, HANDS), ((0, 256), (1, 4)), -0.2, 0.2), 0.0, 1.0).astype(jnp.bfloat16),
        "strategy": jnp.clip(0.049804688 + 0.9501953 * jax.random.uniform(streams_of[4], (BOARDS, RIVERS, LEAVES, HANDS), jnp.float32) ** levels(streams_of[4], (BOARDS, RIVERS, LEAVES, HANDS), ((0, 256), (2, 4)), -0.2, 0.2), 0.049804688, 1.0).astype(jnp.bfloat16),
        "parent_node": draw_parent_node(jax.random.fold_in(streams_of[8], 71), 0),
        "pot_size": jnp.clip(jnp.exp(math.log(4.0) - 2.0794415 * jax.random.uniform(streams_of[6], (LEAVES,), jnp.float32) ** levels(streams_of[6], (LEAVES,), ((0, 4),), -0.2, 0.2)), 0.5, 4.0),
        "flop_weight": jnp.clip(jnp.exp(math.log(10.0) - 4.6051702 * jax.random.uniform(streams_of[7], (BOARDS,), jnp.float32) ** levels(streams_of[7], (BOARDS,), ((0, 256),), -0.2, 0.2)), 0.1, 10.0),
    }


lowest = -1.0e9


def hand_tables():
    card_low, card_high = np.triu_indices(DECK, 1)
    return jnp.asarray(card_low, jnp.int32), jnp.asarray(card_high, jnp.int32)


def unblocked_mask(board_row, card_low, card_high):
    card_hit = (card_low[:, None] == board_row[None, :]) | (card_high[:, None] == board_row[None, :])
    return jnp.where(jnp.any(card_hit, axis=1), 0.0, 1.0).astype(jnp.float32)


def reference(board_cards, hand_ranks, river_count, reach_in, strategy, parent_node, pot_size, flop_weight):
    card_low, card_high = hand_tables()
    shared_card = ((card_low[:, None] == card_low[None, :]) | (card_low[:, None] == card_high[None, :])
                   | (card_high[:, None] == card_low[None, :]) | (card_high[:, None] == card_high[None, :]))
    member = parent_node[:, None] == jnp.arange(NODES, dtype=jnp.int32)[None, :]

    def river_board(board_row, ranking, strat_rows, reach_rows):
        hand_live = unblocked_mask(board_row, card_low, card_high)
        lookup = reach_rows[parent_node].astype(jnp.float32)
        leaf_reach = (lookup * strat_rows.astype(jnp.float32) * hand_live[None, :]).astype(jnp.bfloat16)
        payoff = jnp.where(shared_card, 0, jnp.sign(ranking[:, None] - ranking[None, :])).astype(jnp.bfloat16)
        showdown = jnp.dot(leaf_reach, payoff.T, preferred_element_type=jnp.float32)
        leaf_value = pot_size[:, None] * showdown * hand_live[None, :] / HANDS

        def one_node(column):
            return jnp.max(jnp.where(column[:, None], leaf_value, lowest), axis=0)

        return lax.map(one_node, member.T)

    def flop_group(operands):
        board_rows, rank_rows, strat_all, reach_rows, live_count = operands

        def one_river(inner):
            river_index, board_row, ranking, strat_rows = inner
            return lax.cond(river_index < live_count,
                            lambda: river_board(board_row, ranking, strat_rows, reach_rows),
                            lambda: jnp.zeros((NODES, HANDS), jnp.float32))

        values = lax.map(one_river, (jnp.arange(RIVERS, dtype=jnp.int32), board_rows, rank_rows, strat_all))
        river_live = jnp.arange(RIVERS, dtype=jnp.int32) < live_count
        summed = jnp.sum(jnp.where(river_live[:, None, None], values, 0.0), axis=0)
        return summed / live_count.astype(jnp.float32)

    turn_value = lax.map(flop_group, (board_cards, hand_ranks, strategy, reach_in, river_count))
    root_value = jnp.sum(flop_weight[:, None, None] * turn_value / BOARDS, axis=0)
    return turn_value, root_value
```

```python
import jax
import jax.numpy as jnp
import numpy as np
from jax import lax
from jax.experimental import pallas as pl
from jax.experimental.pallas import tpu as pltpu
from jax.sharding import PartitionSpec as P

HANDS, NODES, RIVERS, LEAF = 1326, 24, 6, 48
NX, NY, NZ, NC = 4, 8, 16, 2
GROUP = NY * NC
SLOTS = 8 * NODES
PART = NODES // NX
TILES = -(-HANDS // 128)
lowest = -1000000000.0
MESH = pl.DeviceIdType.MESH
VM = pl.BlockSpec(memory_space=pltpu.VMEM)
SM = pl.BlockSpec(memory_space=pltpu.SMEM)
f32, bf16 = jnp.float32, jnp.bfloat16


def seq_peer(d):
    return (lax.axis_index("board"), lax.rem(lax.axis_index("seq") + d, NX))


def place():
    board = lax.axis_index("board")
    core = lax.rem(board, NC)
    z = lax.rem(board // NC, NZ)
    return board // (NC * NZ), z, core


def group_peer(d):
    y, z, core = place()
    g = lax.rem(y * NC + core + d, GROUP)
    return ((g // NC * NZ + z) * NC + lax.rem(g, NC), lax.axis_index("seq"))


def line_peer(d):
    y, z, core = place()
    return ((y * NZ + lax.rem(z + d, NZ)) * NC + core, lax.axis_index("seq"))


def meet(peers):
    barrier = pltpu.get_barrier_semaphore()
    for peer in peers:
        pl.semaphore_signal(barrier, inc=1, device_id=peer, device_id_type=MESH)
    pl.semaphore_wait(barrier, len(peers))


def send(src, dst, send_sem, recv_sem, peer):
    copy = pltpu.make_async_remote_copy(
        src_ref=src, dst_ref=dst, send_sem=send_sem, recv_sem=recv_sem, device_id=peer, device_id_type=MESH
    )
    copy.start()
    return copy


def gather_kernel(reach_ref, out_ref, got_ref, send_sem, recv_sem):
    meet([seq_peer(d) for d in range(1, NX)])
    x = lax.axis_index("seq")
    copies = [
        send(reach_ref.at[0], got_ref.at[x], send_sem.at[d], recv_sem.at[d], seq_peer(d)) for d in range(1, NX)
    ]
    got_ref[x] = reach_ref[0]
    for copy in copies:
        copy.wait()
    for x in range(NX):
        out_ref[PART * x : PART * (x + 1), :] = got_ref[x].astype(f32)


def gather(reach):
    return pl.pallas_call(
        gather_kernel,
        name="gather_reach",
        out_shape=jax.ShapeDtypeStruct((NODES, HANDS), f32),
        in_specs=[VM],
        out_specs=VM,
        scratch_shapes=[
            pltpu.VMEM((NX, PART, HANDS), bf16),
            pltpu.SemaphoreType.DMA((NX,)),
            pltpu.SemaphoreType.DMA((NX,)),
        ],
        compiler_params=pltpu.CompilerParams(collective_id=0, has_side_effects=True),
    )(reach)


def compute_kernel(
    cards_ref,
    ranks_ref,
    count_ref,
    reach_ref,
    strat_ref,
    parow_ref,
    pacol_ref,
    pot_ref,
    tab_ref,
    out_ref,
    m_ref,
    row_ref,
    col_ref,
    oh_ref,
    potb_ref,
    biasb_ref,
    scale_ref,
):
    low = tab_ref[0:1, :]
    high = tab_ref[1:2, :]
    card = lax.broadcasted_iota(jnp.int32, (64, HANDS), 0)
    onehot = jnp.where((card == low) | (card == high), 1.0, 0.0).astype(bf16)
    for j in range(0, HANDS, 256):
        w = min(256, HANDS - j)
        shared = lax.dot_general(
            onehot, onehot[:, j : j + w], (((0,), (0,)), ((), ())), preferred_element_type=f32
        )
        m_ref[:, j : j + w] = (1.0 - jnp.minimum(shared, 1.0)).astype(bf16)
    ranks = ranks_ref[...]
    top = ranks // 128
    row_ref[0, 0:RIVERS, :] = (top * 128).astype(f32)
    row_ref[1, 0:RIVERS, :] = (ranks - top * 128).astype(f32)
    col_ref[0] = row_ref[0].T
    col_ref[1] = row_ref[1].T
    cards = cards_ref[...]
    hit = jnp.zeros((RIVERS, HANDS), jnp.bool_)
    for i in range(5):
        hit = hit | (low == cards[:, i : i + 1]) | (high == cards[:, i : i + 1])
    dead = lax.broadcasted_iota(jnp.int32, (RIVERS, HANDS), 0) >= count_ref[0]
    share = 1.0 / (HANDS * jnp.full((RIVERS, HANDS), count_ref[0], jnp.int32).astype(f32))
    scale_ref[0:RIVERS, :] = jnp.where(hit, 0.0, 1.0)
    scale_ref[8 : 8 + RIVERS, :] = jnp.where(hit | dead, 0.0, share)
    prow = parow_ref[...]
    pcol = pacol_ref[...]
    si = lax.broadcasted_iota(jnp.int32, (LEAF, LEAF), 0)
    sj = lax.broadcasted_iota(jnp.int32, (LEAF, LEAF), 1)
    before = jnp.sum(jnp.where((prow == pcol) & (si < sj), 1.0, 0.0), axis=0, keepdims=True).astype(jnp.int32)
    oh = lax.broadcasted_iota(jnp.int32, (SLOTS, LEAF), 0) == before * NODES + prow
    oh_ref[...] = jnp.where(oh, 1.0, 0.0).astype(bf16)
    pot = jnp.sum(jnp.where(oh, pot_ref[...], 0.0), axis=1, keepdims=True)
    used = jnp.sum(jnp.where(oh, 1.0, 0.0), axis=1, keepdims=True)
    potb_ref[...] = jnp.broadcast_to(pot, (SLOTS, 128))
    biasb_ref[...] = jnp.broadcast_to(jnp.where(used > 0.5, 0.0, lowest), (SLOTS, 128))

    reach = reach_ref[...]
    pot2 = jnp.concatenate([potb_ref[...]] * 2, axis=1)
    bias2 = jnp.concatenate([biasb_ref[...]] * 2, axis=1)
    for r in range(RIVERS):
        leaf = jnp.dot(oh_ref[...], strat_ref[r], preferred_element_type=f32).reshape(8, NODES, HANDS)
        leaf = (leaf * (reach * scale_ref[r : r + 1, :])[None]).reshape(SLOTS, HANDS).astype(bf16)
        hc = jnp.broadcast_to(col_ref[0, :HANDS, r : r + 1], (HANDS, 256)).astype(bf16)
        lc = jnp.broadcast_to(col_ref[1, :HANDS, r : r + 1], (HANDS, 256)).astype(bf16)
        for j in range(0, HANDS, 256):
            w = min(256, HANDS - j)
            hr = row_ref[0, r : r + 1, j : j + w].astype(bf16)
            lr = row_ref[1, r : r + 1, j : j + w].astype(bf16)
            gap = (hr - hc[:, :w]) + (lr - lc[:, :w])
            m = m_ref[:, j : j + w]
            payoff = jnp.maximum(jnp.minimum(gap, m), -m)
            val = jnp.dot(leaf, payoff, preferred_element_type=f32)
            val = (val * pot2[:, :w] + bias2[:, :w]).reshape(8, NODES, w)
            best = jnp.max(val, axis=0) * scale_ref[8 + r : 9 + r, j : j + w]
            for x in range(NX):
                out_ref[x, r, :, j : j + w] = best[PART * x : PART * (x + 1)]


def compute(cards, ranks, count, reach, strat, parent, pot):
    tab = jnp.asarray(np.stack(np.triu_indices(52, 1)), jnp.int32)
    return pl.pallas_call(
        compute_kernel,
        name="river_maxima",
        out_shape=jax.ShapeDtypeStruct((NX, RIVERS, PART, HANDS), f32),
        in_specs=[VM, VM, SM, VM, VM, VM, VM, VM, VM],
        out_specs=VM,
        scratch_shapes=[
            pltpu.VMEM((HANDS, HANDS), bf16),
            pltpu.VMEM((2, 8, HANDS), f32),
            pltpu.VMEM((2, HANDS, 8), f32),
            pltpu.VMEM((SLOTS, LEAF), bf16),
            pltpu.VMEM((SLOTS, 128), f32),
            pltpu.VMEM((SLOTS, 128), f32),
            pltpu.VMEM((16, HANDS), f32),
        ],
        compiler_params=pltpu.CompilerParams(vmem_limit_bytes=48 << 20),
    )(cards, ranks, count, reach, strat, parent[None, :], parent[:, None], pot[None, :], tab)


def reduce_kernel(
    part_ref, weight_ref, turn_ref, root_ref, got_ref, mine_ref, in1_ref, sum1_ref, in2_ref, sum2_ref, in3_ref,
    sx, rx, s1, r1, s2, r2, s3, r3,
):
    meet(
        [seq_peer(d) for d in range(1, NX)]
        + [group_peer(d) for d in range(1, GROUP)]
        + [line_peer(d) for d in range(1, NZ)]
    )
    x = lax.axis_index("seq")
    y, z, core = place()
    g = y * NC + core
    copies = [
        send(part_ref.at[lax.rem(x + d, NX)], got_ref.at[d], sx.at[d], rx.at[d], seq_peer(d)) for d in range(1, NX)
    ]
    mine_ref[...] = jnp.zeros_like(mine_ref)
    for copy in copies:
        copy.wait()
    best = jnp.maximum(jnp.maximum(part_ref[x], got_ref[1]), jnp.maximum(got_ref[2], got_ref[3])) if NX == 4 else jnp.maximum(part_ref[x], got_ref[1])
    turn = jnp.sum(best, axis=0)
    turn_ref[...] = turn
    turn = turn * (weight_ref[0] / (NY * NZ * NC))
    for j in range(TILES):
        w = min(128, HANDS - 128 * j)
        mine_ref[j, 0:PART, 0:w] = turn[:, 128 * j : 128 * j + w]
    copies = [
        send(mine_ref.at[lax.rem(g + d, GROUP)], in1_ref.at[d], s1.at[d], r1.at[d], group_peer(d))
        for d in range(1, GROUP)
    ]
    total = mine_ref[g]
    for d in range(1, GROUP):
        copies[d - 1].wait_recv()
        total = total + in1_ref[d]
    sum1_ref[...] = total
    for copy in copies:
        copy.wait_send()
    copies = [send(sum1_ref, in2_ref.at[z], s2.at[d], r2.at[d], line_peer(d)) for d in range(1, NZ)]
    in2_ref[z] = total
    for copy in copies:
        copy.wait()
    sum2_ref[...] = jnp.sum(in2_ref[...], axis=0)
    copies = [send(sum2_ref, in3_ref.at[g], s3.at[d], r3.at[d], group_peer(d)) for d in range(1, GROUP)]
    in3_ref[g] = sum2_ref[...]
    for copy in copies:
        copy.wait()
    for j in range(TILES):
        w = min(128, HANDS - 128 * j)
        root_ref[:, 128 * j : 128 * j + w] = in3_ref[j, 0:PART, 0:w]


def reduce(part, weight):
    tile = (8, 128)
    sems = [pltpu.SemaphoreType.DMA((n,)) for n in (NX, NX, GROUP, GROUP, NZ, NZ, GROUP, GROUP)]
    return pl.pallas_call(
        reduce_kernel,
        name="exchange_reduce",
        out_shape=(jax.ShapeDtypeStruct((PART, HANDS), f32), jax.ShapeDtypeStruct((PART, HANDS), f32)),
        in_specs=[VM, SM],
        out_specs=(VM, VM),
        scratch_shapes=[
            pltpu.VMEM((NX, RIVERS, PART, HANDS), f32),
            pltpu.VMEM((GROUP,) + tile, f32),
            pltpu.VMEM((GROUP,) + tile, f32),
            pltpu.VMEM(tile, f32),
            pltpu.VMEM((NZ,) + tile, f32),
            pltpu.VMEM(tile, f32),
            pltpu.VMEM((GROUP,) + tile, f32),
        ]
        + sems,
        compiler_params=pltpu.CompilerParams(collective_id=1, has_side_effects=True),
    )(part, weight)


def body(
    board_cards, hand_ranks, river_count, reach_in, strategy, parent_node, pot_size, flop_weight
):
    reach = gather(reach_in)
    part = compute(board_cards[0], hand_ranks[0], river_count, reach, strategy[0], parent_node, pot_size)
    turn, root = reduce(part, flop_weight)
    return (turn[None], root)


def solution(mesh):
    return jax.shard_map(
        body,
        mesh=mesh,
        in_specs=(
            P("board", None, None),
            P("board", None, None),
            P("board"),
            P("board", "seq", None),
            P("board", None, "seq", None),
            P("seq"),
            P("seq"),
            P("board"),
        ),
        out_specs=(P("board", "seq", None), P("seq", None)),
        check_vma=False,
    )
```

```python
import jax
import jax.numpy as jnp
import numpy as np
from jax import lax
from jax.experimental import pallas as pl
from jax.experimental.pallas import tpu as pltpu
from jax.sharding import PartitionSpec as P

HANDS, NODES, RIVERS, LEAF = 1326, 24, 6, 48
NX, NY, NZ, NC = 4, 8, 16, 2
GROUP = NY * NC
SLOTS = 8 * NODES
PART = NODES // NX
TILES = -(-HANDS // 128)
lowest = -1000000000.0
MESH = pl.DeviceIdType.MESH
VM = pl.BlockSpec(memory_space=pltpu.VMEM)
HBM = pl.BlockSpec(memory_space=pl.ANY)
SM = pl.BlockSpec(memory_space=pltpu.SMEM)
f32, bf16 = jnp.float32, jnp.bfloat16


def seq_peer(d):
    return (lax.axis_index("board"), lax.rem(lax.axis_index("seq") + d, NX))


def place():
    board = lax.axis_index("board")
    core = lax.rem(board, NC)
    z = lax.rem(board // NC, NZ)
    return board // (NC * NZ), z, core


def group_peer(d):
    y, z, core = place()
    g = lax.rem(y * NC + core + d, GROUP)
    return ((g // NC * NZ + z) * NC + lax.rem(g, NC), lax.axis_index("seq"))


def line_peer(d):
    y, z, core = place()
    return ((y * NZ + lax.rem(z + d, NZ)) * NC + core, lax.axis_index("seq"))


def meet(peers):
    barrier = pltpu.get_barrier_semaphore()
    for peer in peers:
        pl.semaphore_signal(barrier, inc=1, device_id=peer, device_id_type=MESH)
    pl.semaphore_wait(barrier, len(peers))


def send(src, dst, send_sem, recv_sem, peer):
    copy = pltpu.make_async_remote_copy(
        src_ref=src, dst_ref=dst, send_sem=send_sem, recv_sem=recv_sem, device_id=peer, device_id_type=MESH
    )
    copy.start()
    return copy


CHUNK = 256


def far_first(n, width=1):
    return sorted(range(1, n), key=lambda d: -min(d // width, n // width - d // width))


def prepare(tab_ref, mask_ref, rank_ref, row_ref, col_ref, colb_ref, cards_ref, count_ref, scale_ref):
    low = tab_ref[0:1, :]
    high = tab_ref[1:2, :]
    card = lax.broadcasted_iota(jnp.int32, (64, HANDS), 0)
    onehot = jnp.where((card == low) | (card == high), 1.0, 0.0).astype(bf16)
    for j in range(0, HANDS, CHUNK):
        w = min(CHUNK, HANDS - j)
        shared = lax.dot_general(
            onehot, onehot[:, j : j + w], (((0,), (0,)), ((), ())), preferred_element_type=f32
        )
        mask_ref[:, j : j + w] = (1.0 - jnp.minimum(shared, 1.0)).astype(bf16)
    count = jnp.full((1, HANDS), count_ref[0], jnp.int32)
    share = 1.0 / (HANDS * count.astype(f32))
    for r in range(RIVERS):
        row_ref[r : r + 1, :] = rank_ref[r].astype(f32)
        hit = jnp.zeros((1, HANDS), jnp.bool_)
        for i in range(5):
            hit = hit | (low == cards_ref[i, 0, r]) | (high == cards_ref[i, 0, r])
        live = jnp.where(hit, 0.0, 1.0)
        scale_ref[r : r + 1, :] = live
        scale_ref[8 + r : 9 + r, :] = live * jnp.where(count > r, share, 0.0)
    col_ref[...] = row_ref[...].T
    for r in range(RIVERS):
        colb_ref[r] = jnp.broadcast_to(col_ref[:, r : r + 1], (HANDS, 128))


def place_leaves(parent_ref, pot_ref, oh_ref, potb_ref, biasb_ref):
    prow = parent_ref[...]
    si = lax.broadcasted_iota(jnp.int32, (LEAF, LEAF), 0)
    sj = lax.broadcasted_iota(jnp.int32, (LEAF, LEAF), 1)
    pcol = jnp.sum(jnp.where(si == sj, prow.astype(f32), 0.0), axis=1, keepdims=True).astype(jnp.int32)
    before = jnp.sum(jnp.where((prow == pcol) & (si < sj), 1.0, 0.0), axis=0, keepdims=True).astype(jnp.int32)
    oh = lax.broadcasted_iota(jnp.int32, (SLOTS, LEAF), 0) == before * NODES + prow
    oh_ref[...] = jnp.where(oh, 1.0, 0.0).astype(bf16)
    pot = jnp.sum(jnp.where(oh, pot_ref[...], 0.0), axis=1, keepdims=True)
    used = jnp.sum(jnp.where(oh, 1.0, 0.0), axis=1, keepdims=True)
    potb_ref[...] = jnp.broadcast_to(pot, (SLOTS, 128))
    biasb_ref[...] = jnp.broadcast_to(jnp.where(used > 0.5, 0.0, lowest), (SLOTS, 128))


def payoff(r, j, w, row_ref, colb_ref, mask_ref):
    col = jnp.concatenate([colb_ref[r]] * (CHUNK // 128), axis=1)
    gap = row_ref[r : r + 1, j : j + w] - col[:, :w]
    return jnp.clip(gap, -1.0, 1.0).astype(bf16) * mask_ref[:, j : j + w]


def river_kernel(
    cards_ref, count_ref, weight_ref, rank_hbm, reach_hbm, strat_hbm, parent_hbm, pot_hbm, tab_hbm,
    turn_ref, root_ref,
    rank_ref, reach_ref, strat_ref, parent_ref, pot_ref, tab_ref,
    mask_ref, row_ref, col_ref, colb_ref, scale_ref, oh_ref, potb_ref, biasb_ref,
    part_ref, relay_ref, comb_ref, back_ref, ahead_ref, last_ref,
    mine_ref, in1_ref, sum1_ref, in2_ref, sum2_ref, in3_ref,
    local, sg, rg, sa, ra, sb, rb, sc, rc, sl, rl, s1, r1, s2, r2, s3, r3,
):
    x = lax.axis_index("seq")
    y, z, core = place()
    g = y * NC + core
    group_order = far_first(GROUP, NC)
    line_order = far_first(NZ)
    pairs = [(tab_hbm, tab_ref), (rank_hbm, rank_ref), (parent_hbm, parent_ref), (pot_hbm, pot_ref),
             (reach_hbm.at[0], reach_ref.at[x]), (strat_hbm.at[0], strat_ref)]
    fetch = [pltpu.make_async_copy(a, b, local.at[i]) for i, (a, b) in enumerate(pairs)]
    for copy in fetch:
        copy.start()
    peers = [line_peer(d) for d in line_order] + [group_peer(d) for d in group_order]
    peers += [seq_peer(d) for d in (2, 1, 3)]
    barrier = pltpu.get_barrier_semaphore()
    for peer in peers:
        pl.semaphore_signal(barrier, inc=1, device_id=peer, device_id_type=MESH)
    for copy in fetch[:4]:
        copy.wait()
    place_leaves(parent_ref, pot_ref, oh_ref, potb_ref, biasb_ref)
    mine_ref[...] = jnp.zeros_like(mine_ref)
    prepare(tab_ref, mask_ref, rank_ref, row_ref, col_ref, colb_ref, cards_ref, count_ref, scale_ref)
    pl.semaphore_wait(barrier, len(peers))

    copies = [
        send(reach_hbm.at[0], reach_ref.at[x], sg.at[d], rg.at[d], seq_peer(d)) for d in (2, 1, 3)
    ]
    for copy in fetch[4:]:
        copy.wait()
    for copy in copies:
        copy.wait()
    reach = jnp.concatenate([reach_ref[i].astype(f32) for i in range(NX)], axis=0)
    pot2 = jnp.concatenate([potb_ref[...]] * (CHUNK // 128), axis=1)
    bias2 = jnp.concatenate([biasb_ref[...]] * (CHUNK // 128), axis=1)

    def river(r):
        leaf = jnp.dot(oh_ref[...], strat_ref[r], preferred_element_type=f32).reshape(8, NODES, HANDS)
        leaf = (leaf * (reach * scale_ref[r : r + 1, :])[None]).reshape(SLOTS, HANDS).astype(bf16)
        for j in range(0, HANDS, CHUNK):
            w = min(CHUNK, HANDS - j)
            pay = payoff(r, j, w, row_ref, colb_ref, mask_ref)
            val = jnp.dot(leaf, pay, preferred_element_type=f32)
            val = (val * pot2[:, :w] + bias2[:, :w]).reshape(8, NODES, w)
            best = jnp.max(val, axis=0) * scale_ref[8 + r : 9 + r, j : j + w]
            for i in range(NX):
                part_ref[i, r, :, j : j + w] = best[PART * i : PART * (i + 1)]

    def step(r):
        return (1, NX - 1) if r % 2 == 0 else (NX - 1, 1)

    first, direct, second = {}, {}, {}

    def combine(r):
        ahead, behind = step(r)
        first[r].wait_recv()
        comb_ref[r] = jnp.maximum(part_ref[lax.rem(x + ahead, NX), r], relay_ref[r])
        second[r] = send(comb_ref.at[r], ahead_ref.at[r], sc.at[r], rc.at[r], seq_peer(ahead))

    def collect(r):
        direct[r].wait_recv()
        second[r].wait_recv()
        return jnp.maximum(part_ref[x, r], jnp.maximum(back_ref[r], ahead_ref[r]))

    total = jnp.zeros((PART, HANDS), f32)
    end = RIVERS - 1
    for r in range(RIVERS):
        river(r)
        if r < end:
            ahead, behind = step(r)
            first[r] = send(
                part_ref.at[lax.rem(x + 2, NX), r], relay_ref.at[r], sa.at[r], ra.at[r], seq_peer(ahead)
            )
            direct[r] = send(
                part_ref.at[lax.rem(x + behind, NX), r], back_ref.at[r], sb.at[r], rb.at[r], seq_peer(behind)
            )
        else:
            copies = [
                send(part_ref.at[lax.rem(x + d, NX), r], last_ref.at[d - 1], sl.at[d - 1], rl.at[d - 1], seq_peer(d))
                for d in (2, 1, 3)
            ]
        if r >= 1:
            combine(r - 1)
        if r >= 2:
            total = total + collect(r - 2)
    total = total + collect(end - 1)
    for copy in copies:
        copy.wait_recv()
    best = jnp.maximum(part_ref[x, end], jnp.maximum(last_ref[0], jnp.maximum(last_ref[1], last_ref[2])))
    turn = total + best
    share = turn * (weight_ref[0] / (NY * NZ * NC))
    for j in range(TILES):
        w = min(128, HANDS - 128 * j)
        mine_ref[j, 0:PART, 0:w] = share[:, 128 * j : 128 * j + w]
    copies1 = {
        d: send(mine_ref.at[lax.rem(g + d, GROUP)], in1_ref.at[d], s1.at[d], r1.at[d], group_peer(d))
        for d in group_order
    }
    turn_ref[...] = turn
    for d in reversed(group_order):
        copies1[d].wait_recv()
    in1_ref[0] = mine_ref[g]
    part1 = jnp.sum(in1_ref[...], axis=0)
    sum1_ref[...] = part1
    copies2 = [send(sum1_ref, in2_ref.at[z], s2.at[d], r2.at[d], line_peer(d)) for d in line_order]
    in2_ref[z] = part1
    for copy in reversed(copies2):
        copy.wait_recv()
    part2 = jnp.sum(in2_ref[...], axis=0)
    sum2_ref[...] = part2
    copies3 = [send(sum2_ref, in3_ref.at[g], s3.at[d], r3.at[d], group_peer(d)) for d in group_order]
    in3_ref[g] = part2
    for copy in copies:
        copy.wait_send()
    for r in range(end):
        first[r].wait_send()
        direct[r].wait_send()
        second[r].wait_send()
    for copy in list(copies1.values()) + copies2:
        copy.wait_send()
    for copy in reversed(copies3):
        copy.wait()
    for j in range(TILES):
        w = min(128, HANDS - 128 * j)
        root_ref[:, 128 * j : 128 * j + w] = in3_ref[j, 0:PART, 0:w]


def body(
    board_cards, hand_ranks, river_count, reach_in, strategy, parent_node, pot_size, flop_weight
):
    tab = jnp.asarray(np.stack(np.triu_indices(52, 1)), jnp.int32)
    slab = (PART, HANDS)
    tile = (8, 128)
    vm, dma = pltpu.VMEM, pltpu.SemaphoreType.DMA
    scratch = [
        vm((RIVERS, 1, HANDS), jnp.int32),
        vm((NX, PART, HANDS), bf16),
        vm((RIVERS, LEAF, HANDS), bf16),
        vm((1, LEAF), jnp.int32),
        vm((1, LEAF), f32),
        vm((2, HANDS), jnp.int32),
        vm((HANDS, HANDS), bf16),
        vm((8, HANDS), f32),
        vm((HANDS, 8), f32),
        vm((RIVERS, HANDS, 128), f32),
        vm((16, HANDS), f32),
        vm((SLOTS, LEAF), bf16),
        vm((SLOTS, 128), f32),
        vm((SLOTS, 128), f32),
        vm((NX, RIVERS) + slab, f32),
        vm((RIVERS,) + slab, f32),
        vm((RIVERS,) + slab, f32),
        vm((RIVERS,) + slab, f32),
        vm((RIVERS,) + slab, f32),
        vm((NX - 1,) + slab, f32),
        vm((GROUP,) + tile, f32),
        vm((GROUP,) + tile, f32),
        vm(tile, f32),
        vm((NZ,) + tile, f32),
        vm(tile, f32),
        vm((GROUP,) + tile, f32),
    ]
    sems = (6, NX, NX) + (RIVERS,) * 6 + (NX, NX, GROUP, GROUP, NZ, NZ, GROUP, GROUP)
    turn, root = pl.pallas_call(
        river_kernel,
        name="river_values",
        out_shape=(jax.ShapeDtypeStruct(slab, f32), jax.ShapeDtypeStruct(slab, f32)),
        in_specs=[SM, SM, SM] + [HBM] * 6,
        out_specs=(VM, VM),
        scratch_shapes=scratch + [dma((n,)) for n in sems],
        compiler_params=pltpu.CompilerParams(
            collective_id=0, has_side_effects=True, vmem_limit_bytes=60 << 20
        ),
    )(
        jnp.transpose(board_cards, (2, 0, 1)),
        river_count,
        flop_weight,
        jnp.transpose(hand_ranks, (1, 0, 2)),
        reach_in,
        strategy,
        parent_node[None, :],
        pot_size[None, :],
        tab,
    )
    return (turn[None], root)


def solution(mesh):
    return jax.shard_map(
        body,
        mesh=mesh,
        in_specs=(
            P("board", None, None),
            P("board", None, None),
            P("board"),
            P("board", "seq", None),
            P("board", None, "seq", None),
            P("seq"),
            P("seq"),
            P("board"),
        ),
        out_specs=(P("board", "seq", None), P("seq", None)),
        check_vma=False,
    )
```

```python
import jax
import jax.numpy as jnp
import numpy as np
from jax import lax
from jax.experimental import pallas as pl
from jax.experimental.pallas import tpu as pltpu
from jax.sharding import PartitionSpec as P

HANDS, NODES, RIVERS, LEAF = 1326, 24, 6, 48
NX, NY, NZ, NC = 4, 8, 16, 2
GROUP = NY * NC
SLOTS = 8 * NODES
PART = NODES // NX
TILES = -(-HANDS // 128)
lowest = -1000000000.0
MESH = pl.DeviceIdType.MESH
VM = pl.BlockSpec(memory_space=pltpu.VMEM)
HBM = pl.BlockSpec(memory_space=pl.ANY)
SM = pl.BlockSpec(memory_space=pltpu.SMEM)
f32, bf16 = jnp.float32, jnp.bfloat16


def seq_peer(d):
    return (lax.axis_index("board"), lax.rem(lax.axis_index("seq") + d, NX))


def place():
    board = lax.axis_index("board")
    core = lax.rem(board, NC)
    z = lax.rem(board // NC, NZ)
    return board // (NC * NZ), z, core


def group_peer(d):
    y, z, core = place()
    g = lax.rem(y * NC + core + d, GROUP)
    return ((g // NC * NZ + z) * NC + lax.rem(g, NC), lax.axis_index("seq"))


def line_peer(d):
    y, z, core = place()
    return ((y * NZ + lax.rem(z + d, NZ)) * NC + core, lax.axis_index("seq"))


def move(src, dst, send_sem, recv_sem, peer):
    return pltpu.make_async_remote_copy(
        src_ref=src, dst_ref=dst, send_sem=send_sem, recv_sem=recv_sem, device_id=peer, device_id_type=MESH
    )


def send(*args):
    copy = move(*args)
    copy.start()
    return copy


CHUNK = 256


def far_first(n, width=1):
    return sorted(range(1, n), key=lambda d: -min(d // width, n // width - d // width))


def prepare(tab_ref, mask_ref, rank_ref, row_ref, col_ref, colb_ref, cards_ref, count_ref, scale_ref):
    low = tab_ref[0:1, :]
    high = tab_ref[1:2, :]
    card = lax.broadcasted_iota(jnp.int32, (64, HANDS), 0)
    onehot = jnp.where((card == low) | (card == high), 1.0, 0.0).astype(bf16)
    for j in range(0, HANDS, CHUNK):
        w = min(CHUNK, HANDS - j)
        shared = lax.dot_general(
            onehot, onehot[:, j : j + w], (((0,), (0,)), ((), ())), preferred_element_type=f32
        )
        mask_ref[:, j : j + w] = (1.0 - jnp.minimum(shared, 1.0)).astype(bf16)
    count = jnp.full((1, HANDS), count_ref[0], jnp.int32)
    share = 1.0 / (HANDS * count.astype(f32))
    for r in range(RIVERS):
        row_ref[r : r + 1, :] = rank_ref[r].astype(f32)
        hit = jnp.zeros((1, HANDS), jnp.bool_)
        for i in range(5):
            hit = hit | (low == cards_ref[i, 0, r]) | (high == cards_ref[i, 0, r])
        live = jnp.where(hit, 0.0, 1.0)
        scale_ref[r : r + 1, :] = live
        scale_ref[8 + r : 9 + r, :] = live * jnp.where(count > r, share, 0.0)
    col_ref[...] = row_ref[...].T
    for r in range(RIVERS):
        colb_ref[r] = jnp.broadcast_to(col_ref[:, r : r + 1], (HANDS, 128))


def place_leaves(parent_ref, pot_ref, oh_ref, potb_ref, biasb_ref):
    prow = parent_ref[...]
    si = lax.broadcasted_iota(jnp.int32, (LEAF, LEAF), 0)
    sj = lax.broadcasted_iota(jnp.int32, (LEAF, LEAF), 1)
    pcol = jnp.sum(jnp.where(si == sj, prow.astype(f32), 0.0), axis=1, keepdims=True).astype(jnp.int32)
    before = jnp.sum(jnp.where((prow == pcol) & (si < sj), 1.0, 0.0), axis=0, keepdims=True).astype(jnp.int32)
    oh = lax.broadcasted_iota(jnp.int32, (SLOTS, LEAF), 0) == before * NODES + prow
    oh_ref[...] = jnp.where(oh, 1.0, 0.0).astype(bf16)
    pot = jnp.sum(jnp.where(oh, pot_ref[...], 0.0), axis=1, keepdims=True)
    used = jnp.sum(jnp.where(oh, 1.0, 0.0), axis=1, keepdims=True)
    potb_ref[...] = jnp.broadcast_to(pot, (SLOTS, 128))
    biasb_ref[...] = jnp.broadcast_to(jnp.where(used > 0.5, 0.0, lowest), (SLOTS, 128))


def payoff(r, j, w, row_ref, colb_ref, mask_ref):
    col = jnp.concatenate([colb_ref[r]] * (CHUNK // 128), axis=1)
    gap = row_ref[r : r + 1, j : j + w] - col[:, :w]
    return jnp.clip(gap, -1.0, 1.0).astype(bf16) * mask_ref[:, j : j + w]


def river_kernel(
    cards_ref, count_ref, weight_ref, rank_hbm, reach_hbm, strat_hbm, parent_hbm, pot_hbm, tab_hbm,
    turn_ref, root_ref,
    rank_ref, reach_ref, strat_ref, parent_ref, pot_ref, tab_ref,
    mask_ref, row_ref, col_ref, colb_ref, scale_ref, oh_ref, potb_ref, biasb_ref,
    part_ref, relay_ref, comb_ref, back_ref, ahead_ref, last_ref,
    mine_ref, in1_ref, sum1_ref, in2_ref, sum2_ref, in3_ref,
    known_y, known_z, known_far, local, sg, rg, sa, ra, sb, rb, sc, rc, sl, rl, s1, r1, s2, r2, s3, r3,
):
    x = lax.axis_index("seq")
    y, z, core = place()
    g = y * NC + core
    group_order = far_first(GROUP, NC)
    line_order = far_first(NZ)
    pairs = [(tab_hbm, tab_ref), (rank_hbm, rank_ref), (parent_hbm, parent_ref), (pot_hbm, pot_ref),
             (reach_hbm.at[0], reach_ref.at[x]), (strat_hbm.at[0], strat_ref)]
    fetch = [pltpu.make_async_copy(a, b, local.at[i]) for i, (a, b) in enumerate(pairs)]
    for copy in fetch:
        copy.start()
    near = [d for d in group_order if abs(d - GROUP * (d > GROUP // 2)) // NC <= 2]
    peers = [line_peer(d) for d in (2, NZ - 2, 1, NZ - 1)] + [group_peer(d) for d in near]
    peers += [seq_peer(d) for d in (2, 1, 3)]
    barrier = pltpu.get_barrier_semaphore()
    for peer in peers:
        pl.semaphore_signal(barrier, inc=1, device_id=peer, device_id_type=MESH)
    for copy in fetch[:4]:
        copy.wait()
    place_leaves(parent_ref, pot_ref, oh_ref, potb_ref, biasb_ref)
    pl.semaphore_wait(barrier, len(peers))
    copies = [
        send(reach_hbm.at[0], reach_ref.at[x], sg.at[d], rg.at[d], seq_peer(d)) for d in (2, 1, 3)
    ]
    for sem, peer in ((known_y, group_peer(2 * NC)), (known_y, group_peer(GROUP - 2 * NC)),
                      (known_z, line_peer(2)), (known_z, line_peer(NZ - 2))):
        pl.semaphore_signal(sem, inc=1, device_id=peer, device_id_type=MESH)
    prepare(tab_ref, mask_ref, rank_ref, row_ref, col_ref, colb_ref, cards_ref, count_ref, scale_ref)
    mine_ref[...] = jnp.zeros_like(mine_ref)
    for copy in fetch[4:]:
        copy.wait()
    for copy in copies:
        copy.wait()
    reach = jnp.concatenate([reach_ref[i].astype(f32) for i in range(NX)], axis=0)
    pot2 = jnp.concatenate([potb_ref[...]] * (CHUNK // 128), axis=1)
    bias2 = jnp.concatenate([biasb_ref[...]] * (CHUNK // 128), axis=1)

    def river(r):
        leaf = jnp.dot(oh_ref[...], strat_ref[r], preferred_element_type=f32).reshape(8, NODES, HANDS)
        leaf = (leaf * (reach * scale_ref[r : r + 1, :])[None]).reshape(SLOTS, HANDS).astype(bf16)
        for j in range(0, HANDS, CHUNK):
            w = min(CHUNK, HANDS - j)
            pay = payoff(r, j, w, row_ref, colb_ref, mask_ref)
            val = jnp.dot(leaf, pay, preferred_element_type=f32)
            val = (val * pot2[:, :w] + bias2[:, :w]).reshape(8, NODES, w)
            best = jnp.max(val, axis=0) * scale_ref[8 + r : 9 + r, j : j + w]
            for i in range(NX):
                part_ref[i, r, :, j : j + w] = best[PART * i : PART * (i + 1)]

    def step(r):
        return (NX - 1, 1) if r % 2 == 0 else (1, NX - 1)

    first, direct, second = {}, {}, {}

    def combine(r):
        ahead, behind = step(r)
        first[r].wait_recv()
        comb_ref[r] = jnp.maximum(part_ref[lax.rem(x + ahead, NX), r], relay_ref[r])
        second[r] = send(comb_ref.at[r], ahead_ref.at[r], sc.at[r], rc.at[r], seq_peer(ahead))

    def collect(r):
        direct[r].wait_recv()
        second[r].wait_recv()
        return jnp.maximum(part_ref[x, r], jnp.maximum(back_ref[r], ahead_ref[r]))

    total = jnp.zeros((PART, HANDS), f32)
    end = RIVERS - 1
    for r in range(RIVERS):
        river(r)
        if r == 1:
            pl.semaphore_wait(known_y, 2)
            pl.semaphore_wait(known_z, 2)
            for peer in (line_peer(4), line_peer(NZ - 4)):
                pl.semaphore_signal(known_far, inc=1, device_id=peer, device_id_type=MESH)
        if r == 4:
            pl.semaphore_wait(known_far, 2)
        if r < end:
            ahead, behind = step(r)
            first[r] = send(
                part_ref.at[lax.rem(x + 2, NX), r], relay_ref.at[r], sa.at[r], ra.at[r], seq_peer(ahead)
            )
            direct[r] = send(
                part_ref.at[lax.rem(x + behind, NX), r], back_ref.at[r], sb.at[r], rb.at[r], seq_peer(behind)
            )
        else:
            copies = [
                send(part_ref.at[lax.rem(x + d, NX), r], last_ref.at[d - 1], sl.at[d - 1], rl.at[d - 1], seq_peer(d))
                for d in (2, 1, 3)
            ]
        if r >= 2:
            combine(r - 2)
        if r >= 4:
            total = total + collect(r - 4)
    combine(end - 1)
    for r in range(end - 3, end):
        total = total + collect(r)
    for copy in copies:
        copy.wait_recv()
    best = jnp.maximum(part_ref[x, end], jnp.maximum(last_ref[0], jnp.maximum(last_ref[1], last_ref[2])))
    turn = total + best
    share = turn * (weight_ref[0] / (NY * NZ * NC))
    for j in range(TILES):
        w = min(128, HANDS - 128 * j)
        mine_ref[j, :, 0:w] = share[:, 128 * j : 128 * j + w]

    def other(d):
        return lax.rem(g + d, GROUP)

    copies1 = {
        d: move(mine_ref.at[other(d)], in1_ref.at[d], s1.at[d], r1.at[d], group_peer(d)) for d in group_order
    }
    copies2 = [move(sum1_ref, in2_ref.at[z], s2.at[d], r2.at[d], line_peer(d)) for d in line_order]
    copies3 = {d: move(sum2_ref, in3_ref.at[g], s3.at[d], r3.at[d], group_peer(d)) for d in group_order}
    for d in group_order:
        pl.when(other(d) < TILES)(copies1[d].start)
    for i in range(PART):
        turn_ref[i] = turn[i : i + 1]

    @pl.when(g < TILES)
    def _():
        in1_ref[0] = mine_ref[g]
        for d in reversed(group_order):
            copies1[d].wait_recv()
        part1 = jnp.sum(in1_ref[...], axis=0)
        sum1_ref[...] = part1
        for copy in copies2:
            copy.start()
        in2_ref[z] = part1
        for copy in reversed(copies2):
            copy.wait_recv()
        part2 = jnp.sum(in2_ref[...], axis=0)
        sum2_ref[...] = part2
        for d in group_order:
            copies3[d].start()
        in3_ref[g] = part2
        for copy in copies2:
            copy.wait_send()
        for d in group_order:
            copies3[d].wait_send()

    for copy in copies:
        copy.wait_send()
    for r in range(end):
        first[r].wait_send()
        direct[r].wait_send()
        second[r].wait_send()
    for d in group_order:
        pl.when(other(d) < TILES)(copies1[d].wait_send)
    for d in reversed(group_order):
        pl.when(other(GROUP - d) < TILES)(copies3[d].wait_recv)
    for j in range(TILES):
        w = min(128, HANDS - 128 * j)
        root_ref[:, 128 * j : 128 * j + w] = in3_ref[j, :, 0:w]


def body(
    board_cards, hand_ranks, river_count, reach_in, strategy, parent_node, pot_size, flop_weight
):
    tab = jnp.asarray(np.stack(np.triu_indices(52, 1)), jnp.int32)
    slab = (PART, HANDS)
    tile = (PART, 128)
    vm, dma = pltpu.VMEM, pltpu.SemaphoreType.DMA
    scratch = [
        vm((RIVERS, 1, HANDS), jnp.int32),
        vm((NX, PART, HANDS), bf16),
        vm((RIVERS, LEAF, HANDS), bf16),
        vm((1, LEAF), jnp.int32),
        vm((1, LEAF), f32),
        vm((2, HANDS), jnp.int32),
        vm((HANDS, HANDS), bf16),
        vm((8, HANDS), f32),
        vm((HANDS, 8), f32),
        vm((RIVERS, HANDS, 128), f32),
        vm((16, HANDS), f32),
        vm((SLOTS, LEAF), bf16),
        vm((SLOTS, 128), f32),
        vm((SLOTS, 128), f32),
        vm((NX, RIVERS) + slab, f32),
        vm((RIVERS,) + slab, f32),
        vm((RIVERS,) + slab, f32),
        vm((RIVERS,) + slab, f32),
        vm((RIVERS,) + slab, f32),
        vm((NX - 1,) + slab, f32),
        vm((GROUP,) + tile, f32),
        vm((GROUP,) + tile, f32),
        vm(tile, f32),
        vm((NZ,) + tile, f32),
        vm(tile, f32),
        vm((GROUP,) + tile, f32),
    ]
    sems = (6, NX, NX) + (RIVERS,) * 6 + (NX, NX, GROUP, GROUP, NZ, NZ, GROUP, GROUP)
    turn, root = pl.pallas_call(
        river_kernel,
        name="river_values",
        out_shape=(jax.ShapeDtypeStruct((PART, 1, HANDS), f32), jax.ShapeDtypeStruct(slab, f32)),
        in_specs=[SM, SM, SM] + [HBM] * 6,
        out_specs=(VM, VM),
        scratch_shapes=scratch + [pltpu.SemaphoreType.REGULAR] * 3 + [dma((n,)) for n in sems],
        compiler_params=pltpu.CompilerParams(
            collective_id=0, has_side_effects=True, vmem_limit_bytes=60 << 20
        ),
    )(
        jnp.transpose(board_cards, (2, 0, 1)),
        river_count,
        flop_weight,
        jnp.transpose(hand_ranks, (1, 0, 2)),
        reach_in,
        strategy,
        parent_node[None, :],
        pot_size[None, :],
        tab,
    )
    return (jnp.transpose(turn, (1, 0, 2)), root)


def solution(mesh):
    return jax.shard_map(
        body,
        mesh=mesh,
        in_specs=(
            P("board", None, None),
            P("board", None, None),
            P("board"),
            P("board", "seq", None),
            P("board", None, "seq", None),
            P("seq"),
            P("seq"),
            P("board"),
        ),
        out_specs=(P("board", "seq", None), P("seq", None)),
        check_vma=False,
    )
```

```python
import jax
import jax.numpy as jnp
import numpy as np
from jax import lax
from jax.experimental import pallas as pl
from jax.experimental.pallas import tpu as pltpu
from jax.sharding import PartitionSpec as P

HANDS, NODES, RIVERS, LEAF = 1326, 24, 6, 48
NX, NY, NZ, NC = 4, 8, 16, 2
GROUP = NY * NC
SLOTS = 8 * NODES
PART = NODES // NX
WIDE = 1152
REST = HANDS - WIDE
TILES = WIDE // 128
lowest = -1000000000.0
MESH = pl.DeviceIdType.MESH
VM = pl.BlockSpec(memory_space=pltpu.VMEM)
HBM = pl.BlockSpec(memory_space=pl.ANY)
SM = pl.BlockSpec(memory_space=pltpu.SMEM)
f32, bf16 = jnp.float32, jnp.bfloat16


def seq_peer(d):
    return (lax.axis_index("board"), lax.rem(lax.axis_index("seq") + d, NX))


def place():
    board = lax.axis_index("board")
    core = lax.rem(board, NC)
    z = lax.rem(board // NC, NZ)
    return board // (NC * NZ), z, core


def group_peer(d):
    y, z, core = place()
    g = lax.rem(y * NC + core + d, GROUP)
    return ((g // NC * NZ + z) * NC + lax.rem(g, NC), lax.axis_index("seq"))


def line_peer(d):
    y, z, core = place()
    return ((y * NZ + lax.rem(z + d, NZ)) * NC + core, lax.axis_index("seq"))


def move(src, dst, send_sem, recv_sem, peer):
    return pltpu.make_async_remote_copy(
        src_ref=src, dst_ref=dst, send_sem=send_sem, recv_sem=recv_sem, device_id=peer, device_id_type=MESH
    )


def send(*args):
    copy = move(*args)
    copy.start()
    return copy


CHUNK = 256
CHUNKS = [(j, CHUNK) for j in range(0, 1024, CHUNK)] + [(1024, 128), (WIDE, REST)]


def far_first(n, width=1):
    return sorted(range(1, n), key=lambda d: -min(d // width, n // width - d // width))


def prepare(tab_ref, mask_ref, rank_ref, row_ref, col_ref, colb_ref, cards_ref, count_ref, scale_ref):
    low = tab_ref[0:1, :]
    high = tab_ref[1:2, :]
    card = lax.broadcasted_iota(jnp.int32, (64, HANDS), 0)
    onehot = jnp.where((card == low) | (card == high), 1.0, 0.0).astype(bf16)
    for j in range(0, HANDS, CHUNK):
        w = min(CHUNK, HANDS - j)
        shared = lax.dot_general(
            onehot, onehot[:, j : j + w], (((0,), (0,)), ((), ())), preferred_element_type=f32
        )
        mask_ref[:, j : j + w] = (1.0 - jnp.minimum(shared, 1.0)).astype(bf16)
    count = jnp.full((1, HANDS), count_ref[0], jnp.int32)
    share = 1.0 / (HANDS * count.astype(f32))
    for r in range(RIVERS):
        row_ref[r : r + 1, :] = rank_ref[r].astype(f32)
        hit = jnp.zeros((1, HANDS), jnp.bool_)
        for i in range(5):
            hit = hit | (low == cards_ref[i, 0, r]) | (high == cards_ref[i, 0, r])
        live = jnp.where(hit, 0.0, 1.0)
        scale_ref[r : r + 1, :] = live
        scale_ref[8 + r : 9 + r, :] = live * jnp.where(count > r, share, 0.0)
    col_ref[...] = row_ref[...].T
    for r in range(RIVERS):
        colb_ref[r] = jnp.broadcast_to(col_ref[:, r : r + 1], (HANDS, 128))


def place_leaves(parent_ref, pot_ref, oh_ref, potb_ref, biasb_ref):
    prow = parent_ref[...]
    si = lax.broadcasted_iota(jnp.int32, (LEAF, LEAF), 0)
    sj = lax.broadcasted_iota(jnp.int32, (LEAF, LEAF), 1)
    pcol = jnp.sum(jnp.where(si == sj, prow.astype(f32), 0.0), axis=1, keepdims=True).astype(jnp.int32)
    before = jnp.sum(jnp.where((prow == pcol) & (si < sj), 1.0, 0.0), axis=0, keepdims=True).astype(jnp.int32)
    oh = lax.broadcasted_iota(jnp.int32, (SLOTS, LEAF), 0) == before * NODES + prow
    oh_ref[...] = jnp.where(oh, 1.0, 0.0).astype(bf16)
    pot = jnp.sum(jnp.where(oh, pot_ref[...], 0.0), axis=1, keepdims=True)
    used = jnp.sum(jnp.where(oh, 1.0, 0.0), axis=1, keepdims=True)
    potb_ref[...] = jnp.broadcast_to(pot, (SLOTS, 128))
    biasb_ref[...] = jnp.broadcast_to(jnp.where(used > 0.5, 0.0, lowest), (SLOTS, 128))


def spare(i):
    return PART + i // 4, i % 4 * 256


def payoff(r, j, w, row_ref, colb_ref, mask_ref):
    col = jnp.concatenate([colb_ref[r]] * (CHUNK // 128), axis=1)
    gap = row_ref[r : r + 1, j : j + w] - col[:, :w]
    return jnp.clip(gap, -1.0, 1.0).astype(bf16) * mask_ref[:, j : j + w]


def river_kernel(
    cards_hbm, count_ref, weight_ref, rank_hbm, reach_hbm, strat_hbm, parent_hbm, pot_hbm, tab_hbm,
    turn_ref, root_ref,
    cards_ref, rank_ref, reach_ref, strat_ref, parent_ref, pot_ref, tab_ref,
    pay_ref, mask_ref, row_ref, col_ref, colb_ref, scale_ref, oh_ref, potb_ref, biasb_ref,
    part_ref, relay_ref, comb_ref, back_ref, ahead_ref, last_ref,
    mine_ref, in1_ref, sum1_ref, in2_ref, sum2_ref, in3_ref,
    known_y, known_z, known_far, local, sg, rg, sa, ra, sb, rb, sc, rc, sl, rl, s1, r1, s2, r2, s3, r3,
):
    x = lax.axis_index("seq")
    y, z, core = place()
    g = y * NC + core
    group_order = far_first(GROUP, NC)
    line_order = far_first(NZ)
    pairs = [(cards_hbm, cards_ref), (tab_hbm, tab_ref), (rank_hbm, rank_ref), (parent_hbm, parent_ref), (pot_hbm, pot_ref),
             (reach_hbm.at[0], reach_ref.at[x]), (strat_hbm.at[0], strat_ref)]
    fetch = [pltpu.make_async_copy(a, b, local.at[i]) for i, (a, b) in enumerate(pairs)]
    for copy in fetch:
        copy.start()
    near = [d for d in group_order if abs(d - GROUP * (d > GROUP // 2)) // NC <= 2]
    peers = [line_peer(d) for d in (2, NZ - 2, 1, NZ - 1)] + [group_peer(d) for d in near]
    peers += [seq_peer(d) for d in (2, 1, 3)]
    barrier = pltpu.get_barrier_semaphore()
    for peer in peers:
        pl.semaphore_signal(barrier, inc=1, device_id=peer, device_id_type=MESH)
    for copy in fetch[:5]:
        copy.wait()
    place_leaves(parent_ref, pot_ref, oh_ref, potb_ref, biasb_ref)
    pl.semaphore_wait(barrier, len(peers))
    copies = [
        send(reach_hbm.at[0], reach_ref.at[x], sg.at[d], rg.at[d], seq_peer(d)) for d in (2, 1, 3)
    ]
    for sem, peer in ((known_y, group_peer(2 * NC)), (known_y, group_peer(GROUP - 2 * NC)),
                      (known_z, line_peer(2)), (known_z, line_peer(NZ - 2))):
        pl.semaphore_signal(sem, inc=1, device_id=peer, device_id_type=MESH)
    prepare(tab_ref, mask_ref, rank_ref, row_ref, col_ref, colb_ref, cards_ref, count_ref, scale_ref)
    part_ref[:, :, PART:8, :] = jnp.zeros((NX, RIVERS, 8 - PART, WIDE), f32)
    for j, w in CHUNKS:
        pay_ref[:, j : j + w] = payoff(0, j, w, row_ref, colb_ref, mask_ref)
    for copy in fetch[5:]:
        copy.wait()
    for copy in copies:
        copy.wait()
    reach = jnp.concatenate([reach_ref[i].astype(f32) for i in range(NX)], axis=0)
    pot2 = jnp.concatenate([potb_ref[...]] * (CHUNK // 128), axis=1)
    bias2 = jnp.concatenate([biasb_ref[...]] * (CHUNK // 128), axis=1)

    def river(r):
        leaf = jnp.dot(oh_ref[...], strat_ref[r], preferred_element_type=f32).reshape(8, NODES, HANDS)
        leaf = (leaf * (reach * scale_ref[r : r + 1, :])[None]).reshape(SLOTS, HANDS).astype(bf16)
        for j, w in CHUNKS:
            if r == 0:
                pay = pay_ref[:, j : j + w]
            else:
                pay = payoff(r, j, w, row_ref, colb_ref, mask_ref)
            val = jnp.dot(leaf, pay, preferred_element_type=f32)
            val = (val * pot2[:, :w] + bias2[:, :w]).reshape(8, NODES, w)
            best = jnp.max(val, axis=0) * scale_ref[8 + r : 9 + r, j : j + w]
            for i in range(NX):
                if j < WIDE:
                    part_ref[i, r, 0:PART, j : j + w] = best[PART * i : PART * (i + 1)]
                else:
                    for k in range(PART):
                        row, at = spare(k)
                        part_ref[i, r, row : row + 1, at : at + w] = best[PART * i + k : PART * i + k + 1]

    def step(r):
        return (NX - 1, 1) if r % 2 == 0 else (1, NX - 1)

    first, direct, second = {}, {}, {}

    def combine(r):
        ahead, behind = step(r)
        first[r].wait_recv()
        comb_ref[r] = jnp.maximum(part_ref[lax.rem(x + ahead, NX), r], relay_ref[r])
        second[r] = send(comb_ref.at[r], ahead_ref.at[r], sc.at[r], rc.at[r], seq_peer(ahead))

    def collect(r):
        direct[r].wait_recv()
        second[r].wait_recv()
        return jnp.maximum(part_ref[x, r], jnp.maximum(back_ref[r], ahead_ref[r]))

    total = jnp.zeros((8, WIDE), f32)
    end = RIVERS - 1
    for r in range(RIVERS):
        river(r)
        if r == 1:
            pl.semaphore_wait(known_y, 2)
            pl.semaphore_wait(known_z, 2)
            for peer in (line_peer(4), line_peer(NZ - 4)):
                pl.semaphore_signal(known_far, inc=1, device_id=peer, device_id_type=MESH)
        if r == 4:
            pl.semaphore_wait(known_far, 2)
        if r < end:
            ahead, behind = step(r)
            first[r] = send(
                part_ref.at[lax.rem(x + 2, NX), r], relay_ref.at[r], sa.at[r], ra.at[r], seq_peer(ahead)
            )
            direct[r] = send(
                part_ref.at[lax.rem(x + behind, NX), r], back_ref.at[r], sb.at[r], rb.at[r], seq_peer(behind)
            )
        else:
            copies = [
                send(part_ref.at[lax.rem(x + d, NX), r], last_ref.at[d - 1], sl.at[d - 1], rl.at[d - 1], seq_peer(d))
                for d in (2, 1, 3)
            ]
        if r >= 2:
            combine(r - 2)
        if r >= 4:
            total = total + collect(r - 4)
    combine(end - 1)
    for r in range(end - 3, end):
        total = total + collect(r)
    for copy in copies:
        copy.wait_recv()
    best = jnp.maximum(part_ref[x, end], jnp.maximum(last_ref[0], jnp.maximum(last_ref[1], last_ref[2])))
    turn = total + best
    share = turn * (weight_ref[0] / (NY * NZ * NC))
    for j in range(TILES):
        mine_ref[j] = share[:, 128 * j : 128 * (j + 1)]

    def other(d):
        return lax.rem(g + d, GROUP)

    copies1 = {
        d: move(mine_ref.at[other(d)], in1_ref.at[d], s1.at[d], r1.at[d], group_peer(d)) for d in group_order
    }
    copies2 = [move(sum1_ref, in2_ref.at[z], s2.at[d], r2.at[d], line_peer(d)) for d in line_order]
    copies3 = {d: move(sum2_ref, in3_ref.at[g], s3.at[d], r3.at[d], group_peer(d)) for d in group_order}
    for d in group_order:
        pl.when(other(d) < TILES)(copies1[d].start)
    for i in range(PART):
        row, at = spare(i)
        turn_ref[i, :, 0:WIDE] = turn[i : i + 1]
        turn_ref[i, :, WIDE:HANDS] = turn[row : row + 1, at : at + REST]

    @pl.when(g < TILES)
    def _():
        in1_ref[0] = mine_ref[g]
        for d in reversed(group_order):
            copies1[d].wait_recv()
        part1 = jnp.sum(in1_ref[...], axis=0)
        sum1_ref[...] = part1
        for copy in copies2:
            copy.start()
        in2_ref[z] = part1
        for copy in reversed(copies2):
            copy.wait_recv()
        part2 = jnp.sum(in2_ref[...], axis=0)
        sum2_ref[...] = part2
        for d in group_order:
            copies3[d].start()
        in3_ref[g] = part2
        for copy in copies2:
            copy.wait_send()
        for d in group_order:
            copies3[d].wait_send()

    for copy in copies:
        copy.wait_send()
    for r in range(end):
        first[r].wait_send()
        direct[r].wait_send()
        second[r].wait_send()
    for d in group_order:
        pl.when(other(d) < TILES)(copies1[d].wait_send)
    for d in reversed(group_order):
        pl.when(other(GROUP - d) < TILES)(copies3[d].wait_recv)
    for j in range(TILES):
        root_ref[:, 128 * j : 128 * (j + 1)] = in3_ref[j, 0:PART, :]
    for i in range(PART):
        row, at = spare(i)
        root_ref[i : i + 1, WIDE : WIDE + 128] = in3_ref[at // 128, row : row + 1, :]
        root_ref[i : i + 1, WIDE + 128 : HANDS] = in3_ref[at // 128 + 1, row : row + 1, 0 : REST - 128]


def body(
    board_cards, hand_ranks, river_count, reach_in, strategy, parent_node, pot_size, flop_weight
):
    tab = jnp.asarray(np.stack(np.triu_indices(52, 1)), jnp.int32)
    slab = (8, WIDE)
    tile = (8, 128)
    vm, dma = pltpu.VMEM, pltpu.SemaphoreType.DMA
    scratch = [
        pltpu.SMEM((5, 1, RIVERS), jnp.int32),
        vm((RIVERS, 1, HANDS), jnp.int32),
        vm((NX, PART, HANDS), bf16),
        vm((RIVERS, LEAF, HANDS), bf16),
        vm((1, LEAF), jnp.int32),
        vm((1, LEAF), f32),
        vm((2, HANDS), jnp.int32),
        vm((HANDS, HANDS), bf16),
        vm((HANDS, HANDS), bf16),
        vm((8, HANDS), f32),
        vm((HANDS, 8), f32),
        vm((RIVERS, HANDS, 128), f32),
        vm((16, HANDS), f32),
        vm((SLOTS, LEAF), bf16),
        vm((SLOTS, 128), f32),
        vm((SLOTS, 128), f32),
        vm((NX, RIVERS) + slab, f32),
        vm((RIVERS,) + slab, f32),
        vm((RIVERS,) + slab, f32),
        vm((RIVERS,) + slab, f32),
        vm((RIVERS,) + slab, f32),
        vm((NX - 1,) + slab, f32),
        vm((GROUP,) + tile, f32),
        vm((GROUP,) + tile, f32),
        vm(tile, f32),
        vm((NZ,) + tile, f32),
        vm(tile, f32),
        vm((GROUP,) + tile, f32),
    ]
    sems = (7, NX, NX) + (RIVERS,) * 6 + (NX, NX, GROUP, GROUP, NZ, NZ, GROUP, GROUP)
    turn, root = pl.pallas_call(
        river_kernel,
        name="river_values",
        out_shape=(jax.ShapeDtypeStruct((PART, 1, HANDS), f32), jax.ShapeDtypeStruct((PART, HANDS), f32)),
        in_specs=[HBM, SM, SM] + [HBM] * 6,
        out_specs=(VM, VM),
        scratch_shapes=scratch + [pltpu.SemaphoreType.REGULAR] * 3 + [dma((n,)) for n in sems],
        compiler_params=pltpu.CompilerParams(
            collective_id=0, has_side_effects=True, vmem_limit_bytes=60 << 20
        ),
    )(
        jnp.transpose(board_cards, (2, 0, 1)),
        river_count,
        flop_weight,
        jnp.transpose(hand_ranks, (1, 0, 2)),
        reach_in,
        strategy,
        parent_node[None, :],
        pot_size[None, :],
        tab,
    )
    return (jnp.transpose(turn, (1, 0, 2)), root)


def solution(mesh):
    return jax.shard_map(
        body,
        mesh=mesh,
        in_specs=(
            P("board", None, None),
            P("board", None, None),
            P("board"),
            P("board", "seq", None),
            P("board", None, "seq", None),
            P("seq"),
            P("seq"),
            P("board"),
        ),
        out_specs=(P("board", "seq", None), P("seq", None)),
        check_vma=False,
    )
```

```python
import jax
import jax.numpy as jnp
import numpy as np
from jax import lax
from jax.experimental import pallas as pl
from jax.experimental.pallas import tpu as pltpu
from jax.sharding import PartitionSpec as P

HANDS, NODES, RIVERS, LEAF = 1326, 24, 6, 48
NX, NY, NZ, NC = 4, 8, 16, 2
GROUP = NY * NC
SLOTS = 8 * NODES
PART = NODES // NX
WIDE = 1024
REST = HANDS - WIDE
TILES = WIDE // 128
lowest = -1000000000.0
MESH = pl.DeviceIdType.MESH
VM = pl.BlockSpec(memory_space=pltpu.VMEM)
HBM = pl.BlockSpec(memory_space=pl.ANY)
SM = pl.BlockSpec(memory_space=pltpu.SMEM)
f32, bf16 = jnp.float32, jnp.bfloat16


def seq_peer(d):
    return (lax.axis_index("board"), lax.rem(lax.axis_index("seq") + d, NX))


def place():
    board = lax.axis_index("board")
    core = lax.rem(board, NC)
    z = lax.rem(board // NC, NZ)
    return board // (NC * NZ), z, core


def group_peer(d):
    y, z, core = place()
    g = lax.rem(y * NC + core + d, GROUP)
    return ((g // NC * NZ + z) * NC + lax.rem(g, NC), lax.axis_index("seq"))


def line_peer(d):
    y, z, core = place()
    return ((y * NZ + lax.rem(z + d, NZ)) * NC + core, lax.axis_index("seq"))


def move(src, dst, send_sem, recv_sem, peer):
    return pltpu.make_async_remote_copy(
        src_ref=src, dst_ref=dst, send_sem=send_sem, recv_sem=recv_sem, device_id=peer, device_id_type=MESH
    )


def send(*args):
    copy = move(*args)
    copy.start()
    return copy


CHUNK = 256
CHUNKS = [(j, CHUNK) for j in range(0, WIDE, CHUNK)] + [(WIDE, REST)]


def far_first(n, width=1):
    return sorted(range(1, n), key=lambda d: -min(d // width, n // width - d // width))


def prepare(tab_ref, mask_ref, rank_ref, row_ref, col_ref, colb_ref, cards_ref, count_ref, scale_ref):
    low = tab_ref[0:1, :]
    high = tab_ref[1:2, :]
    card = lax.broadcasted_iota(jnp.int32, (64, HANDS), 0)
    onehot = jnp.where((card == low) | (card == high), 1.0, 0.0).astype(bf16)
    for j in range(0, HANDS, CHUNK):
        w = min(CHUNK, HANDS - j)
        shared = lax.dot_general(
            onehot, onehot[:, j : j + w], (((0,), (0,)), ((), ())), preferred_element_type=f32
        )
        mask_ref[:, j : j + w] = (1.0 - jnp.minimum(shared, 1.0)).astype(bf16)
    count = jnp.full((1, HANDS), count_ref[0], jnp.int32)
    for r in range(RIVERS):
        row_ref[r : r + 1, :] = rank_ref[r].astype(f32)
        hit = jnp.zeros((1, HANDS), jnp.bool_)
        for i in range(5):
            hit = hit | (low == cards_ref[i, 0, r]) | (high == cards_ref[i, 0, r])
        live = jnp.where(hit, 0.0, 1.0)
        scale_ref[r : r + 1, :] = live
        scale_ref[8 + r : 9 + r, :] = live * jnp.where(count > r, 1.0 / HANDS, 0.0)
    col_ref[...] = row_ref[...].T
    for r in range(RIVERS):
        colb_ref[r] = jnp.broadcast_to(col_ref[:, r : r + 1], (HANDS, 128))


def place_leaves(parent_ref, pot_ref, oh_ref, potb_ref, biasb_ref):
    prow = parent_ref[...]
    si = lax.broadcasted_iota(jnp.int32, (LEAF, LEAF), 0)
    sj = lax.broadcasted_iota(jnp.int32, (LEAF, LEAF), 1)
    pcol = jnp.sum(jnp.where(si == sj, prow.astype(f32), 0.0), axis=1, keepdims=True).astype(jnp.int32)
    before = jnp.sum(jnp.where((prow == pcol) & (si < sj), 1.0, 0.0), axis=0, keepdims=True).astype(jnp.int32)
    oh = lax.broadcasted_iota(jnp.int32, (SLOTS, LEAF), 0) == before * NODES + prow
    oh_ref[...] = jnp.where(oh, 1.0, 0.0).astype(bf16)
    pot = jnp.sum(jnp.where(oh, pot_ref[...], 0.0), axis=1, keepdims=True)
    used = jnp.sum(jnp.where(oh, 1.0, 0.0), axis=1, keepdims=True)
    potb_ref[...] = jnp.broadcast_to(pot, (SLOTS, 128))
    biasb_ref[...] = jnp.broadcast_to(jnp.where(used > 0.5, 0.0, lowest), (SLOTS, 128))


def spare(i):
    return PART + i // 3, i % 3 * REST


def payoff(r, j, w, row_ref, colb_ref, mask_ref):
    col = jnp.concatenate([colb_ref[r]] * 3, axis=1)
    gap = row_ref[r : r + 1, j : j + w] - col[:, :w]
    return jnp.clip(gap, -1.0, 1.0).astype(bf16) * mask_ref[:, j : j + w]


def river_kernel(
    cards_hbm, count_ref, weight_ref, rank_hbm, reach_hbm, strat_hbm, parent_hbm, pot_hbm, tab_hbm,
    turn_ref, root_ref,
    cards_ref, rank_ref, reach_ref, strat_ref, parent_ref, pot_ref, tab_ref,
    pay_ref, mask_ref, row_ref, col_ref, colb_ref, scale_ref, oh_ref, potb_ref, biasb_ref,
    part_ref, relay_ref, comb_ref, back_ref, ahead_ref, last_ref,
    flat_ref, mine_ref, in1_ref, sum1_ref, in2_ref, sum2_ref, in3_ref,
    known_y, known_z, known_far, local, sg, rg, sa, ra, sb, rb, sc, rc, sl, rl, s1, r1, s2, r2, s3, r3,
):
    x = lax.axis_index("seq")
    y, z, core = place()
    g = y * NC + core
    group_order = far_first(GROUP, NC)
    line_order = far_first(NZ)
    pairs = [(cards_hbm, cards_ref), (tab_hbm, tab_ref), (rank_hbm, rank_ref), (parent_hbm, parent_ref), (pot_hbm, pot_ref),
             (reach_hbm.at[0], reach_ref.at[x]), (strat_hbm.at[0], strat_ref)]
    fetch = [pltpu.make_async_copy(a, b, local.at[i]) for i, (a, b) in enumerate(pairs)]
    for copy in fetch:
        copy.start()
    near = [d for d in group_order if abs(d - GROUP * (d > GROUP // 2)) // NC <= 2]
    peers = [line_peer(d) for d in (2, NZ - 2, 1, NZ - 1)] + [group_peer(d) for d in near]
    peers += [seq_peer(d) for d in (2, 1, 3)]
    barrier = pltpu.get_barrier_semaphore()
    for peer in peers:
        pl.semaphore_signal(barrier, inc=1, device_id=peer, device_id_type=MESH)
    for copy in fetch[:5]:
        copy.wait()
    place_leaves(parent_ref, pot_ref, oh_ref, potb_ref, biasb_ref)
    pl.semaphore_wait(barrier, len(peers))
    copies = [
        send(reach_hbm.at[0], reach_ref.at[x], sg.at[d], rg.at[d], seq_peer(d)) for d in (2, 1, 3)
    ]
    for sem, peer in ((known_y, group_peer(2 * NC)), (known_y, group_peer(GROUP - 2 * NC)),
                      (known_z, line_peer(2)), (known_z, line_peer(NZ - 2))):
        pl.semaphore_signal(sem, inc=1, device_id=peer, device_id_type=MESH)
    prepare(tab_ref, mask_ref, rank_ref, row_ref, col_ref, colb_ref, cards_ref, count_ref, scale_ref)
    part_ref[:, :, PART:8, :] = jnp.zeros((NX, RIVERS, 8 - PART, WIDE), f32)
    for j, w in CHUNKS:
        pay_ref[:, j : j + w] = payoff(0, j, w, row_ref, colb_ref, mask_ref)
    for copy in fetch[5:]:
        copy.wait()
    for copy in copies:
        copy.wait()
    reach = jnp.concatenate([reach_ref[i].astype(f32) for i in range(NX)], axis=0)
    pot2 = jnp.concatenate([potb_ref[...]] * 3, axis=1)
    bias2 = jnp.concatenate([biasb_ref[...]] * 3, axis=1)

    def river(r):
        leaf = jnp.dot(oh_ref[...], strat_ref[r], preferred_element_type=f32).reshape(8, NODES, HANDS)
        leaf = (leaf * (reach * scale_ref[r : r + 1, :])[None]).reshape(SLOTS, HANDS).astype(bf16)
        for j, w in CHUNKS:
            if r == 0:
                pay = pay_ref[:, j : j + w]
            else:
                pay = payoff(r, j, w, row_ref, colb_ref, mask_ref)
            val = jnp.dot(leaf, pay, preferred_element_type=f32)
            val = (val * pot2[:, :w] + bias2[:, :w]).reshape(8, NODES, w)
            best = jnp.max(val, axis=0) * scale_ref[8 + r : 9 + r, j : j + w]
            for i in range(NX):
                if j < WIDE:
                    part_ref[i, r, 0:PART, j : j + w] = best[PART * i : PART * (i + 1)]
                else:
                    for k in range(PART):
                        row, at = spare(k)
                        part_ref[i, r, row : row + 1, at : at + w] = best[PART * i + k : PART * i + k + 1]

    def step(r):
        return (NX - 1, 1) if r % 2 == 0 else (1, NX - 1)

    first, direct, second = {}, {}, {}

    def combine(r):
        ahead, behind = step(r)
        first[r].wait_recv()
        comb_ref[r] = jnp.maximum(part_ref[lax.rem(x + ahead, NX), r], relay_ref[r])
        second[r] = send(comb_ref.at[r], ahead_ref.at[r], sc.at[r], rc.at[r], seq_peer(ahead))

    def collect(r):
        direct[r].wait_recv()
        second[r].wait_recv()
        return jnp.maximum(part_ref[x, r], jnp.maximum(back_ref[r], ahead_ref[r]))

    total = jnp.zeros((8, WIDE), f32)
    end = RIVERS - 1
    for r in range(RIVERS):
        river(r)
        if r == 1:
            pl.semaphore_wait(known_y, 2)
            pl.semaphore_wait(known_z, 2)
            for peer in (line_peer(4), line_peer(NZ - 4)):
                pl.semaphore_signal(known_far, inc=1, device_id=peer, device_id_type=MESH)
        if r == 4:
            pl.semaphore_wait(known_far, 2)
        if r < end:
            ahead, behind = step(r)
            first[r] = send(
                part_ref.at[lax.rem(x + 2, NX), r], relay_ref.at[r], sa.at[r], ra.at[r], seq_peer(ahead)
            )
            direct[r] = send(
                part_ref.at[lax.rem(x + behind, NX), r], back_ref.at[r], sb.at[r], rb.at[r], seq_peer(behind)
            )
        else:
            copies = [
                send(part_ref.at[lax.rem(x + d, NX), r], last_ref.at[d - 1], sl.at[d - 1], rl.at[d - 1], seq_peer(d))
                for d in (2, 1, 3)
            ]
        if r >= 2:
            combine(r - 2)
        if r >= 4:
            total = total + collect(r - 4)
    combine(end - 1)
    for r in range(end - 3, end):
        total = total + collect(r)
    for copy in copies:
        copy.wait_recv()
    best = jnp.maximum(part_ref[x, end], jnp.maximum(last_ref[0], jnp.maximum(last_ref[1], last_ref[2])))
    turn = total + best
    share = turn * (weight_ref[0] / count_ref[0].astype(f32))
    for j in range(TILES):
        mine_ref[j] = share[:, 128 * j : 128 * (j + 1)]

    def other(d):
        return lax.rem(g + d, GROUP)

    copies1 = {
        d: move(mine_ref.at[other(d)], in1_ref.at[d], s1.at[d], r1.at[d], group_peer(d)) for d in group_order
    }
    copies2 = [move(sum1_ref, in2_ref.at[z], s2.at[d], r2.at[d], line_peer(d)) for d in line_order]
    copies3 = {d: move(sum2_ref, in3_ref.at[g], s3.at[d], r3.at[d], group_peer(d)) for d in group_order}
    for d in group_order:
        pl.when(other(d) < TILES)(copies1[d].start)
    flat_ref[...] = turn
    for i in range(PART):
        row, at = spare(i)
        turn_ref[i, :, 0:WIDE] = turn[i : i + 1]
        turn_ref[i, :, WIDE:HANDS] = flat_ref[row : row + 1, at : at + REST]

    @pl.when(g < TILES)
    def _():
        in1_ref[0] = mine_ref[g]
        for d in reversed(group_order):
            copies1[d].wait_recv()
        part1 = jnp.sum(in1_ref[...], axis=0)
        sum1_ref[...] = part1
        for copy in copies2:
            copy.start()
        in2_ref[z] = part1
        for copy in reversed(copies2):
            copy.wait_recv()
        part2 = jnp.sum(in2_ref[...], axis=0)
        sum2_ref[...] = part2
        for d in group_order:
            copies3[d].start()
        in3_ref[g] = part2
        for copy in copies2:
            copy.wait_send()
        for d in group_order:
            copies3[d].wait_send()

    for copy in copies:
        copy.wait_send()
    for r in range(end):
        first[r].wait_send()
        direct[r].wait_send()
        second[r].wait_send()
    for d in group_order:
        pl.when(other(d) < TILES)(copies1[d].wait_send)
    for d in reversed(group_order):
        pl.when(other(GROUP - d) < TILES)(copies3[d].wait_recv)
    for j in range(TILES):
        root_ref[:, 128 * j : 128 * (j + 1)] = in3_ref[j, 0:PART, :]
        flat_ref[PART:8, 128 * j : 128 * (j + 1)] = in3_ref[j, PART:8, :]
    for i in range(PART):
        row, at = spare(i)
        root_ref[i : i + 1, WIDE:HANDS] = flat_ref[row : row + 1, at : at + REST]


def body(
    board_cards, hand_ranks, river_count, reach_in, strategy, parent_node, pot_size, flop_weight
):
    tab = jnp.asarray(np.stack(np.triu_indices(52, 1)), jnp.int32)
    slab = (8, WIDE)
    tile = (8, 128)
    vm, dma = pltpu.VMEM, pltpu.SemaphoreType.DMA
    scratch = [
        pltpu.SMEM((5, 1, RIVERS), jnp.int32),
        vm((RIVERS, 1, HANDS), jnp.int32),
        vm((NX, PART, HANDS), bf16),
        vm((RIVERS, LEAF, HANDS), bf16),
        vm((1, LEAF), jnp.int32),
        vm((1, LEAF), f32),
        vm((2, HANDS), jnp.int32),
        vm((HANDS, HANDS), bf16),
        vm((HANDS, HANDS), bf16),
        vm((8, HANDS), f32),
        vm((HANDS, 8), f32),
        vm((RIVERS, HANDS, 128), f32),
        vm((16, HANDS), f32),
        vm((SLOTS, LEAF), bf16),
        vm((SLOTS, 128), f32),
        vm((SLOTS, 128), f32),
        vm((NX, RIVERS) + slab, f32),
        vm((RIVERS,) + slab, f32),
        vm((RIVERS,) + slab, f32),
        vm((RIVERS,) + slab, f32),
        vm((RIVERS,) + slab, f32),
        vm((NX - 1,) + slab, f32),
        vm(slab, f32),
        vm((GROUP,) + tile, f32),
        vm((GROUP,) + tile, f32),
        vm(tile, f32),
        vm((NZ,) + tile, f32),
        vm(tile, f32),
        vm((GROUP,) + tile, f32),
    ]
    sems = (7, NX, NX) + (RIVERS,) * 6 + (NX, NX, GROUP, GROUP, NZ, NZ, GROUP, GROUP)
    turn, root = pl.pallas_call(
        river_kernel,
        name="river_values",
        out_shape=(jax.ShapeDtypeStruct((PART, 1, HANDS), f32), jax.ShapeDtypeStruct((PART, HANDS), f32)),
        in_specs=[HBM, SM, SM] + [HBM] * 6,
        out_specs=(VM, VM),
        scratch_shapes=scratch + [pltpu.SemaphoreType.REGULAR] * 3 + [dma((n,)) for n in sems],
        compiler_params=pltpu.CompilerParams(
            collective_id=0, has_side_effects=True, vmem_limit_bytes=60 << 20
        ),
    )(
        jnp.transpose(board_cards, (2, 0, 1)),
        river_count,
        flop_weight,
        jnp.transpose(hand_ranks, (1, 0, 2)),
        reach_in,
        strategy,
        parent_node[None, :],
        pot_size[None, :],
        tab,
    )
    return (jnp.transpose(turn, (1, 0, 2)) / river_count[0].astype(f32), root / (NY * NZ * NC))


def solution(mesh):
    return jax.shard_map(
        body,
        mesh=mesh,
        in_specs=(
            P("board", None, None),
            P("board", None, None),
            P("board"),
            P("board", "seq", None),
            P("board", None, "seq", None),
            P("seq"),
            P("seq"),
            P("board"),
        ),
        out_specs=(P("board", "seq", None), P("seq", None)),
        check_vma=False,
    )
```

```python
import jax
import jax.numpy as jnp
import numpy as np
from jax import lax
from jax.experimental import pallas as pl
from jax.experimental.pallas import tpu as pltpu
from jax.sharding import PartitionSpec as P

HANDS, NODES, RIVERS, LEAF = 1326, 24, 6, 48
NX, NY, NZ, NC = 4, 8, 16, 2
GROUP = NY * NC
SLOTS = 8 * NODES
PART = NODES // NX
WIDE = 1024
REST = HANDS - WIDE
TILES = WIDE // 128
lowest = -1000000000.0
MESH = pl.DeviceIdType.MESH
VM = pl.BlockSpec(memory_space=pltpu.VMEM)
HBM = pl.BlockSpec(memory_space=pl.ANY)
SM = pl.BlockSpec(memory_space=pltpu.SMEM)
f32, bf16 = jnp.float32, jnp.bfloat16


def seq_peer(d):
    return (lax.axis_index("board"), lax.rem(lax.axis_index("seq") + d, NX))


def place():
    board = lax.axis_index("board")
    core = lax.rem(board, NC)
    z = lax.rem(board // NC, NZ)
    return board // (NC * NZ), z, core


def group_peer(d):
    y, z, core = place()
    g = lax.rem(y * NC + core + d, GROUP)
    return ((g // NC * NZ + z) * NC + lax.rem(g, NC), lax.axis_index("seq"))


def line_peer(d):
    y, z, core = place()
    return ((y * NZ + lax.rem(z + d, NZ)) * NC + core, lax.axis_index("seq"))


def move(src, dst, send_sem, recv_sem, peer):
    return pltpu.make_async_remote_copy(
        src_ref=src, dst_ref=dst, send_sem=send_sem, recv_sem=recv_sem, device_id=peer, device_id_type=MESH
    )


def send(*args):
    copy = move(*args)
    copy.start()
    return copy


CHUNK = 256
CHUNKS = [(j, CHUNK) for j in range(0, WIDE, CHUNK)] + [(WIDE, REST)]


def far_first(n, width=1):
    return sorted(range(1, n), key=lambda d: -min(d // width, n // width - d // width))


def prepare(tab_ref, mask_ref, rank_ref, row_ref, col_ref, colb_ref, cards_ref, count_ref, scale_ref):
    low = tab_ref[0:1, :]
    high = tab_ref[1:2, :]
    card = lax.broadcasted_iota(jnp.int32, (64, HANDS), 0)
    onehot = jnp.where((card == low) | (card == high), 1.0, 0.0).astype(bf16)
    for j in range(0, HANDS, CHUNK):
        w = min(CHUNK, HANDS - j)
        shared = lax.dot_general(
            onehot, onehot[:, j : j + w], (((0,), (0,)), ((), ())), preferred_element_type=f32
        )
        mask_ref[:, j : j + w] = (1.0 - jnp.minimum(shared, 1.0)).astype(bf16)
    count = jnp.full((1, HANDS), count_ref[0], jnp.int32)
    for r in range(RIVERS):
        row_ref[r : r + 1, :] = rank_ref[r].astype(f32)
        hit = jnp.zeros((1, HANDS), jnp.bool_)
        for i in range(5):
            hit = hit | (low == cards_ref[i, 0, r]) | (high == cards_ref[i, 0, r])
        live = jnp.where(hit, 0.0, 1.0)
        scale_ref[r : r + 1, :] = live
        scale_ref[8 + r : 9 + r, :] = live * jnp.where(count > r, 1.0 / HANDS, 0.0)
    col_ref[...] = row_ref[...].T
    for r in range(RIVERS):
        colb_ref[r] = jnp.broadcast_to(col_ref[:, r : r + 1], (HANDS, 128))


def place_leaves(parent_ref, pot_ref, oh_ref, potb_ref, biasb_ref):
    prow = parent_ref[...]
    si = lax.broadcasted_iota(jnp.int32, (LEAF, LEAF), 0)
    sj = lax.broadcasted_iota(jnp.int32, (LEAF, LEAF), 1)
    pcol = jnp.sum(jnp.where(si == sj, prow.astype(f32), 0.0), axis=1, keepdims=True).astype(jnp.int32)
    before = jnp.sum(jnp.where((prow == pcol) & (si < sj), 1.0, 0.0), axis=0, keepdims=True).astype(jnp.int32)
    oh = lax.broadcasted_iota(jnp.int32, (SLOTS, LEAF), 0) == before * NODES + prow
    oh_ref[...] = jnp.where(oh, 1.0, 0.0).astype(bf16)
    pot = jnp.sum(jnp.where(oh, pot_ref[...], 0.0), axis=1, keepdims=True)
    used = jnp.sum(jnp.where(oh, 1.0, 0.0), axis=1, keepdims=True)
    potb_ref[...] = jnp.broadcast_to(pot, (SLOTS, 128))
    biasb_ref[...] = jnp.broadcast_to(jnp.where(used > 0.5, 0.0, lowest), (SLOTS, 128))


def spare(i):
    return PART + i // 3, i % 3 * REST


def payoff(r, j, w, row_ref, colb_ref, mask_ref):
    col = jnp.concatenate([colb_ref[r]] * 3, axis=1)
    gap = row_ref[r : r + 1, j : j + w] - col[:, :w]
    return jnp.clip(gap.astype(bf16), -1.0, 1.0) * mask_ref[:, j : j + w]


def river_kernel(
    cards_hbm, count_ref, weight_ref, rank_hbm, reach_hbm, strat_hbm, parent_hbm, pot_hbm, tab_hbm,
    turn_ref, root_ref,
    cards_ref, rank_ref, reach_ref, strat_ref, parent_ref, pot_ref, tab_ref,
    pay_ref, mask_ref, row_ref, col_ref, colb_ref, scale_ref, oh_ref, potb_ref, biasb_ref,
    part_ref, relay_ref, comb_ref, back_ref, ahead_ref, last_ref,
    flat_ref, mine_ref, in1_ref, sum1_ref, in2_ref, sum2_ref, in3_ref,
    known_y, known_z, known_far, local, sg, rg, sa, ra, sb, rb, sc, rc, sl, rl, s1, r1, s2, r2, s3, r3,
):
    x = lax.axis_index("seq")
    y, z, core = place()
    g = y * NC + core
    group_order = far_first(GROUP, NC)
    line_order = far_first(NZ)
    pairs = [(cards_hbm, cards_ref), (tab_hbm, tab_ref), (rank_hbm, rank_ref), (parent_hbm, parent_ref), (pot_hbm, pot_ref),
             (reach_hbm.at[0], reach_ref.at[x]), (strat_hbm.at[0], strat_ref)]
    fetch = [pltpu.make_async_copy(a, b, local.at[i]) for i, (a, b) in enumerate(pairs)]
    for copy in fetch:
        copy.start()
    near = [d for d in group_order if abs(d - GROUP * (d > GROUP // 2)) // NC <= 2]
    peers = [line_peer(d) for d in (2, NZ - 2, 1, NZ - 1)] + [group_peer(d) for d in near]
    peers += [seq_peer(d) for d in (2, 1, 3)]
    barrier = pltpu.get_barrier_semaphore()
    for peer in peers:
        pl.semaphore_signal(barrier, inc=1, device_id=peer, device_id_type=MESH)
    for copy in fetch[:5]:
        copy.wait()
    place_leaves(parent_ref, pot_ref, oh_ref, potb_ref, biasb_ref)
    pl.semaphore_wait(barrier, len(peers))
    copies = [
        send(reach_hbm.at[0], reach_ref.at[x], sg.at[d], rg.at[d], seq_peer(d)) for d in (2, 1, 3)
    ]
    for sem, peer in ((known_y, group_peer(2 * NC)), (known_y, group_peer(GROUP - 2 * NC)),
                      (known_z, line_peer(2)), (known_z, line_peer(NZ - 2))):
        pl.semaphore_signal(sem, inc=1, device_id=peer, device_id_type=MESH)
    prepare(tab_ref, mask_ref, rank_ref, row_ref, col_ref, colb_ref, cards_ref, count_ref, scale_ref)
    part_ref[:, :, PART:8, :] = jnp.zeros((NX, RIVERS, 8 - PART, WIDE), f32)
    for j, w in CHUNKS:
        pay_ref[:, j : j + w] = payoff(0, j, w, row_ref, colb_ref, mask_ref)
    for copy in fetch[5:]:
        copy.wait()
    for copy in copies:
        copy.wait()
    reach = jnp.concatenate([reach_ref[i].astype(f32) for i in range(NX)], axis=0)
    pot2 = jnp.concatenate([potb_ref[...]] * 3, axis=1)
    bias2 = jnp.concatenate([biasb_ref[...]] * 3, axis=1)

    def river(r):
        leaf = jnp.dot(oh_ref[...], strat_ref[r], preferred_element_type=f32).reshape(8, NODES, HANDS)
        leaf = (leaf * (reach * scale_ref[r : r + 1, :])[None]).reshape(SLOTS, HANDS).astype(bf16)
        for j, w in CHUNKS:
            if r == 0:
                pay = pay_ref[:, j : j + w]
            else:
                pay = payoff(r, j, w, row_ref, colb_ref, mask_ref)
            val = jnp.dot(leaf, pay, preferred_element_type=f32)
            val = (val * pot2[:, :w] + bias2[:, :w]).reshape(8, NODES, w)
            best = jnp.max(val, axis=0) * scale_ref[8 + r : 9 + r, j : j + w]
            for i in range(NX):
                if j < WIDE:
                    part_ref[i, r, 0:PART, j : j + w] = best[PART * i : PART * (i + 1)]
                else:
                    for k in range(PART):
                        row, at = spare(k)
                        part_ref[i, r, row : row + 1, at : at + w] = best[PART * i + k : PART * i + k + 1]

    def step(r):
        return (NX - 1, 1) if r % 2 == 0 else (1, NX - 1)

    first, direct, second = {}, {}, {}

    def combine(r):
        ahead, behind = step(r)
        first[r].wait_recv()
        comb_ref[r] = jnp.maximum(part_ref[lax.rem(x + ahead, NX), r], relay_ref[r])
        second[r] = send(comb_ref.at[r], ahead_ref.at[r], sc.at[r], rc.at[r], seq_peer(ahead))

    def collect(r):
        direct[r].wait_recv()
        second[r].wait_recv()
        return jnp.maximum(part_ref[x, r], jnp.maximum(back_ref[r], ahead_ref[r]))

    total = jnp.zeros((8, WIDE), f32)
    end = RIVERS - 1
    for r in range(RIVERS):
        river(r)
        if r == 1:
            pl.semaphore_wait(known_y, 2)
            pl.semaphore_wait(known_z, 2)
            for peer in (line_peer(4), line_peer(NZ - 4)):
                pl.semaphore_signal(known_far, inc=1, device_id=peer, device_id_type=MESH)
        if r == 4:
            pl.semaphore_wait(known_far, 2)
        if r < end:
            ahead, behind = step(r)
            first[r] = send(
                part_ref.at[lax.rem(x + 2, NX), r], relay_ref.at[r], sa.at[r], ra.at[r], seq_peer(ahead)
            )
            direct[r] = send(
                part_ref.at[lax.rem(x + behind, NX), r], back_ref.at[r], sb.at[r], rb.at[r], seq_peer(behind)
            )
        else:
            copies = [
                send(part_ref.at[lax.rem(x + d, NX), r], last_ref.at[d - 1], sl.at[d - 1], rl.at[d - 1], seq_peer(d))
                for d in (2, 1, 3)
            ]
        if r >= 2:
            combine(r - 2)
        if r >= 4:
            total = total + collect(r - 4)
    combine(end - 1)
    for r in range(end - 3, end):
        total = total + collect(r)
    for copy in copies:
        copy.wait_recv()
    best = jnp.maximum(part_ref[x, end], jnp.maximum(last_ref[0], jnp.maximum(last_ref[1], last_ref[2])))
    turn = total + best
    share = turn * (weight_ref[0] / count_ref[0].astype(f32))
    for j in range(TILES):
        mine_ref[j] = share[:, 128 * j : 128 * (j + 1)]

    def other(d):
        return lax.rem(g + d, GROUP)

    copies1 = {
        d: move(mine_ref.at[other(d)], in1_ref.at[d], s1.at[d], r1.at[d], group_peer(d)) for d in group_order
    }
    copies2 = [move(sum1_ref, in2_ref.at[z], s2.at[d], r2.at[d], line_peer(d)) for d in line_order]
    copies3 = {d: move(sum2_ref, in3_ref.at[g], s3.at[d], r3.at[d], group_peer(d)) for d in group_order}
    for d in group_order:
        pl.when(other(d) < TILES)(copies1[d].start)
    flat_ref[...] = turn
    for i in range(PART):
        row, at = spare(i)
        turn_ref[i, :, 0:WIDE] = turn[i : i + 1]
        turn_ref[i, :, WIDE:HANDS] = flat_ref[row : row + 1, at : at + REST]

    @pl.when(g < TILES)
    def _():
        in1_ref[0] = mine_ref[g]
        for d in reversed(group_order):
            copies1[d].wait_recv()
        part1 = jnp.sum(in1_ref[...], axis=0)
        sum1_ref[...] = part1
        for copy in copies2:
            copy.start()
        in2_ref[z] = part1
        for copy in reversed(copies2):
            copy.wait_recv()
        part2 = jnp.sum(in2_ref[...], axis=0)
        sum2_ref[...] = part2
        for d in group_order:
            copies3[d].start()
        in3_ref[g] = part2
        for copy in copies2:
            copy.wait_send()
        for d in group_order:
            copies3[d].wait_send()

    for copy in copies:
        copy.wait_send()
    for r in range(end):
        first[r].wait_send()
        direct[r].wait_send()
        second[r].wait_send()
    for d in group_order:
        pl.when(other(d) < TILES)(copies1[d].wait_send)
    for d in reversed(group_order):
        pl.when(other(GROUP - d) < TILES)(copies3[d].wait_recv)
    for j in range(TILES):
        root_ref[:, 128 * j : 128 * (j + 1)] = in3_ref[j, 0:PART, :]
        flat_ref[PART:8, 128 * j : 128 * (j + 1)] = in3_ref[j, PART:8, :]
    for i in range(PART):
        row, at = spare(i)
        root_ref[i : i + 1, WIDE:HANDS] = flat_ref[row : row + 1, at : at + REST]


def body(
    board_cards, hand_ranks, river_count, reach_in, strategy, parent_node, pot_size, flop_weight
):
    tab = jnp.asarray(np.stack(np.triu_indices(52, 1)), jnp.int32)
    slab = (8, WIDE)
    tile = (8, 128)
    vm, dma = pltpu.VMEM, pltpu.SemaphoreType.DMA
    scratch = [
        pltpu.SMEM((5, 1, RIVERS), jnp.int32),
        vm((RIVERS, 1, HANDS), jnp.int32),
        vm((NX, PART, HANDS), bf16),
        vm((RIVERS, LEAF, HANDS), bf16),
        vm((1, LEAF), jnp.int32),
        vm((1, LEAF), f32),
        vm((2, HANDS), jnp.int32),
        vm((HANDS, HANDS), bf16),
        vm((HANDS, HANDS), bf16),
        vm((8, HANDS), f32),
        vm((HANDS, 8), f32),
        vm((RIVERS, HANDS, 128), f32),
        vm((16, HANDS), f32),
        vm((SLOTS, LEAF), bf16),
        vm((SLOTS, 128), f32),
        vm((SLOTS, 128), f32),
        vm((NX, RIVERS) + slab, f32),
        vm((RIVERS,) + slab, f32),
        vm((RIVERS,) + slab, f32),
        vm((RIVERS,) + slab, f32),
        vm((RIVERS,) + slab, f32),
        vm((NX - 1,) + slab, f32),
        vm(slab, f32),
        vm((GROUP,) + tile, f32),
        vm((GROUP,) + tile, f32),
        vm(tile, f32),
        vm((NZ,) + tile, f32),
        vm(tile, f32),
        vm((GROUP,) + tile, f32),
    ]
    sems = (7, NX, NX) + (RIVERS,) * 6 + (NX, NX, GROUP, GROUP, NZ, NZ, GROUP, GROUP)
    turn, root = pl.pallas_call(
        river_kernel,
        name="river_values",
        out_shape=(jax.ShapeDtypeStruct((PART, 1, HANDS), f32), jax.ShapeDtypeStruct((PART, HANDS), f32)),
        in_specs=[HBM, SM, SM] + [HBM] * 6,
        out_specs=(VM, VM),
        scratch_shapes=scratch + [pltpu.SemaphoreType.REGULAR] * 3 + [dma((n,)) for n in sems],
        compiler_params=pltpu.CompilerParams(
            collective_id=0, has_side_effects=True, vmem_limit_bytes=60 << 20
        ),
    )(
        jnp.transpose(board_cards, (2, 0, 1)),
        river_count,
        flop_weight,
        jnp.transpose(hand_ranks, (1, 0, 2)),
        reach_in,
        strategy,
        parent_node[None, :],
        pot_size[None, :],
        tab,
    )
    return (jnp.transpose(turn, (1, 0, 2)) / river_count[0].astype(f32), root / (NY * NZ * NC))


def solution(mesh):
    return jax.shard_map(
        body,
        mesh=mesh,
        in_specs=(
            P("board", None, None),
            P("board", None, None),
            P("board"),
            P("board", "seq", None),
            P("board", None, "seq", None),
            P("seq"),
            P("seq"),
            P("board"),
        ),
        out_specs=(P("board", "seq", None), P("seq", None)),
        check_vma=False,
    )
```
